32 devices in a mesh: lat: 4 (over z), lon: 8 (over y, x, core).
Axes of the slice: x: 2, y: 2, z: 4, core: 2. Of those that a mesh axis runs over, the one named last changes fastest.
Arguments:
- adjoint_in: float32 [2, 10, 512, 2048], P(None, None, 'lat', 'lon'), may hold values from -6 to 6
- east_flow: float32 [10, 512, 2048], P(None, 'lat', 'lon'), may hold values from -0.2 to 0.2
- north_flow: float32 [10, 512, 2048], P(None, 'lat', 'lon'), may hold values from -0.2 to 0.2
- diffusivity: float32 [2, 10], replicated, may hold values from 0.01 to 0.05
- land_mask: int32 [10, 512, 2048], P(None, 'lat', 'lon'), may hold values 0 or 1
- forcing: bfloat16 [32, 64, 2, 10, 128], P(('lat', 'lon')), may hold values from -6 to 6
- obs_tile: int32 [32, 64], P(('lat', 'lon')), may hold values from 0 to 31, as said below
- obs_block: int32 [32, 64], P(('lat', 'lon')), may hold values from 0 to 255
- obs_live: int32 [32], P(('lat', 'lon')), may hold values from 48 to 64, as said below
Outputs:
- adjoint_out: float32 [2, 10, 512, 2048], P(None, None, 'lat', 'lon')
The draws below stay inside these ranges and needn't reach their ends.
Inputs may be any that keep to these rules, and one draw needn't show every extreme that they name: `obs_tile`: among the live records of one holder no tile is named more than 4 times. Records at positions obs_live[h] and beyond of holder h are not live.
All inputs are finite; a program needn't handle non-finite values. No bound on the sum of `land_mask` on one device may be relied on, other than what follows from the above.
Results may differ from the reference program's by a relative error of at most 0.0017.
Values may be sent and summed in bfloat16 or wider, within the bound.
No kernel may reach another device: no remote copies, remote signals or barrier semaphores. Data moves between devices by JAX's collectives and lax.ppermute only.
A program may use at most 128 MiB of HBM per device.

```python
import math
import jax
import jax.numpy as jnp
from jax import lax

LEV = 10
CLAT = 128
CLON = 256
BW = 128
OBS_PEER = 2
STEPS = 3
OBS_DEV = 64
CBLK = 256
NLAT = 512
NLON = 2048
N_LON = 8
DEVICES = 32


def routing_plan(key):
    base_key = jax.random.fold_in(key, 7)
    key_list = jax.random.split(base_key, 6)
    holders = jnp.arange(DEVICES, dtype=jnp.int32)
    hot_score = jax.random.randint(key_list[0], (DEVICES,), 0, 2 ** 20) * DEVICES + holders
    hot_rank = jnp.sum(hot_score[None, :] > hot_score[:, None], axis=1)
    is_hot = (hot_rank < 4).astype(jnp.int32)
    dest_key = jax.random.randint(key_list[1], (DEVICES, DEVICES), 0, 2 ** 20) * DEVICES + holders[None, :] + is_hot[None, :] * 2 ** 28
    dest_order = jnp.argsort(-dest_key, axis=1).astype(jnp.int32)
    group_sizes = jax.random.randint(key_list[2], (DEVICES, DEVICES), OBS_PEER, 2 * OBS_PEER + 1)
    group_sizes = jnp.where(holders[None, :] < 4, 2 * OBS_PEER, group_sizes)
    group_ends = jnp.cumsum(group_sizes, axis=1)
    sorted_pos = jnp.arange(OBS_DEV, dtype=jnp.int32)
    group_index = jnp.sum(group_ends[:, None, :] <= sorted_pos[None, :, None], axis=2).astype(jnp.int32)
    sorted_tile = jnp.take_along_axis(dest_order, group_index, axis=1)
    live_count = jax.random.randint(key_list[3], (DEVICES,), 3 * OBS_DEV // 4, OBS_DEV + 1)
    full_holder = jax.random.randint(key_list[4], (), 0, DEVICES)
    live_count = jnp.where(holders == full_holder, OBS_DEV, live_count).astype(jnp.int32)
    row_noise = jax.random.randint(key_list[5], (DEVICES, OBS_DEV), 0, 2 ** 12)
    order_key = row_noise * OBS_DEV + sorted_pos[None, :] + jnp.where(sorted_pos[None, :] >= live_count[:, None], 2 ** 28, 0)
    row_order = jnp.argsort(order_key, axis=1)
    dest_tiles = jnp.take_along_axis(sorted_tile, row_order, axis=1)
    return (dest_tiles.astype(jnp.int32), live_count)


def draw_obs_tile(key, part):
    return routing_plan(key)[0]


def draw_obs_live(key, part):
    return routing_plan(key)[1]


def place_ends(values, stream_key, low, high):
    spot = [jax.random.randint(jax.random.fold_in(stream_key, axis), (), 0, length) for axis, length in enumerate(values.shape)]
    main_axis = values.shape.index(max(values.shape))
    neighbour = spot[:main_axis] + [(spot[main_axis] + 1) % values.shape[main_axis]] + spot[main_axis + 1:]
    return values.at[tuple(spot)].set(low).at[tuple(neighbour)].set(high)


def levels(rng, dims, cuts, least, largest):
    def one(position, parts):
        heights = jax.random.uniform(jax.random.fold_in(jax.random.fold_in(rng, 6), position), (parts,), jnp.float32, least / len(cuts), largest / len(cuts))
        return jnp.repeat(jnp.exp(heights), dims[position] // parts).reshape((-1,) + (1,) * (len(dims) - position - 1))

    level = one(*cuts[0])
    for cut in cuts[1:]:
        level = level * one(*cut)
    return level


def noise(own_key, dims, width, reach, cuts=(), held_as=jnp.bfloat16):
    values = jax.random.normal(own_key, dims, jnp.float32) * width
    if len(cuts) > 0:
        values = levels(own_key, dims, cuts, -0.22, 0.18) * values
    return jnp.clip(values, min=-reach, max=reach).astype(held_as)


def setup_inputs(seed: int = 0) -> dict:
    key_of = jax.random.split(jax.random.key(seed), 10)
    adjoint_in = noise(key_of[0], (2, LEV, NLAT, NLON), 1.0, 6.0, ((2, 4), (3, 8)), jnp.float32)
    east_flow = jnp.clip(jax.random.uniform(key_of[1], (LEV, NLAT, NLON), jnp.float32, -0.2, 0.2) * levels(key_of[1], (LEV, NLAT, NLON), ((1, 4), (2, 8)), -0.4, 0.0), -0.2, 0.2)
    north_flow = jnp.clip(jax.random.uniform(key_of[2], (LEV, NLAT, NLON), jnp.float32, -0.2, 0.2) * levels(key_of[2], (LEV, NLAT, NLON), ((1, 4), (2, 8)), -0.4, 0.0), -0.2, 0.2)
    diffusivity = jnp.clip(jnp.exp(jax.random.uniform(key_of[3], (2, LEV), jnp.float32, math.log(0.01), math.log(0.05))), 0.01, 0.05)
    land_mask = place_ends((jax.random.randint(key_of[4], (LEV, NLAT, NLON), 0, 10) < 7).astype(jnp.int32), jax.random.fold_in(key_of[4], 1), 0, 1)
    forcing = noise(key_of[5], (DEVICES, OBS_DEV, 2, LEV, BW), 1.0, 6.0, ((0, 32),))
    obs_tile = draw_obs_tile(jax.random.fold_in(key_of[9], 71), 0)
    obs_block = place_ends(jax.random.randint(key_of[7], (DEVICES, OBS_DEV), 0, CBLK), jax.random.fold_in(key_of[7], 1), 0, CBLK - 1).astype(jnp.int32)
    obs_live = draw_obs_live(jax.random.fold_in(key_of[9], 71), 0)
    return dict(adjoint_in=adjoint_in, east_flow=east_flow, north_flow=north_flow, diffusivity=diffusivity, land_mask=land_mask, forcing=forcing, obs_tile=obs_tile, obs_block=obs_block, obs_live=obs_live)


def forcing_field(forcing, obs_tile, obs_block, obs_live):
    record_index = jnp.arange(OBS_DEV, dtype=jnp.int32)
    live_rows = record_index[None, :] < obs_live[:, None]
    per_row = CLON // BW
    lat_band = obs_tile // N_LON
    column_tile = obs_tile % N_LON
    global_block = (lat_band * CLAT + obs_block // per_row) * (NLON // BW) + column_tile * per_row + obs_block % per_row
    values = jnp.where(live_rows[:, :, None, None, None], forcing.astype(jnp.float32), jnp.zeros((), jnp.float32))
    summed = jax.ops.segment_sum(values.reshape(DEVICES * OBS_DEV, 2, LEV, BW), global_block.reshape(DEVICES * OBS_DEV).astype(jnp.int32), num_segments=NLAT * NLON // BW)
    return summed.reshape(NLAT, NLON // BW, 2, LEV, BW).transpose(2, 3, 0, 1, 4).reshape(2, LEV, NLAT, NLON)


def advance_slice(index, state_flat, east_flow, north_flow, spread_flat, ocean_mask, open_rows):
    level = index % LEV
    field = state_flat[index]
    east_here = east_flow[level]
    north_here = north_flow[level] * open_rows
    spread = spread_flat[index]
    spread_open = spread * open_rows
    ocean_here = ocean_mask[level]
    for repeat in range(STEPS):
        masked = field * ocean_here
        east_gap = jnp.roll(masked, -1, axis=1) - masked
        outflow_x = (jnp.minimum(east_here, 0.0) - spread) * east_gap
        zonal_term = (jnp.maximum(east_here, 0.0) + spread) * east_gap + jnp.roll(outflow_x, 1, axis=1)
        upper = jnp.concatenate([masked[1:], jnp.zeros_like(masked[:1])], axis=0)
        north_gap = upper - masked
        outflow_y = (jnp.minimum(north_here, 0.0) - spread_open) * north_gap
        merid_term = (jnp.maximum(north_here, 0.0) + spread_open) * north_gap + jnp.concatenate([jnp.zeros_like(outflow_y[:1]), outflow_y[:-1]], axis=0)
        field = masked + zonal_term + merid_term
    return field


def reference(adjoint_in, east_flow, north_flow, diffusivity, land_mask, forcing, obs_tile, obs_block, obs_live):
    initial = adjoint_in + forcing_field(forcing, obs_tile, obs_block, obs_live)
    state_flat = initial.reshape(2 * LEV, NLAT, NLON)
    open_rows = (jnp.arange(NLAT) < NLAT - 1).astype(jnp.float32)[:, None]
    spread_flat = diffusivity.reshape(2 * LEV)
    ocean_mask = land_mask.astype(jnp.float32)

    def one_slice(index):
        return advance_slice(index, state_flat, east_flow, north_flow, spread_flat, ocean_mask, open_rows)

    result = lax.map(one_slice, jnp.arange(2 * LEV, dtype=jnp.int32))
    return result.reshape(2, LEV, NLAT, NLON)
```

```python
import functools

import jax
import jax.numpy as jnp
from jax import lax
from jax.experimental import pallas as pl
from jax.experimental.pallas import tpu as pltpu
from jax.sharding import PartitionSpec as P

STEPS = 3
LANES = 128
F32 = jnp.float32
BF16 = jnp.bfloat16
VMEM = pl.BlockSpec(memory_space=pltpu.VMEM)
SMEM = pl.BlockSpec(memory_space=pltpu.SMEM)


def iota(shape, dim):
    return lax.broadcasted_iota(jnp.int32, shape, dim)


def fiota(shape, dim):
    return iota(shape, dim).astype(F32)


def west_lane(shape):
    lane = fiota(shape, 1)
    return lane - 6.0 * jnp.floor((lane + 0.5) / 6.0) < 3.0


def one_hot(rows, code):
    shape = (rows, code.shape[1])
    return jnp.where(fiota(shape, 0) == code, 1.0, 0.0).astype(BF16)


def dot(a, b):
    return jnp.dot(a, b, preferred_element_type=F32)


def pack_body(n_lon, live_ref, tile_ref, block_ref, forcing_ref, out_ref, wide):
    records, levels = forcing_ref.shape[1], forcing_ref.shape[3]
    count = 2 * levels
    devices = out_ref.shape[0]
    tile = tile_ref[...].astype(F32)
    block = block_ref[...].astype(F32)
    square = (records, records)
    low, high = iota(square, 0), iota(square, 1)
    tile_col = jnp.sum(jnp.where(low == high, tile, 0.0), axis=1, keepdims=True)
    block_col = jnp.sum(jnp.where(low == high, block, 0.0), axis=1, keepdims=True)
    earlier = jnp.where((tile_col == tile) & (low < high), 1.0, 0.0)
    rank = jnp.sum(earlier, axis=0, keepdims=True)
    live = iota((1, records), 1) < live_ref[0]
    band = jnp.floor((tile + 0.5) / n_lon) * n_lon
    column = tile - band
    east = band + jnp.where(column == n_lon - 1, 0.0, column + 1.0)
    west = band + jnp.where(column == 0.0, n_lon - 1.0, column - 1.0)
    half = block - 2.0 * jnp.floor(block * 0.5)
    code = jnp.where(live, tile * 8.0 + rank, -8.0)
    to_east = jnp.where(live & (half == 1.0), east * 8.0 + rank, -8.0)
    to_west = jnp.where(live & (half == 0.0), west * 8.0 + rank, -8.0)
    for r in range(records):
        for t in range(2):
            wide[pl.ds(r * 32 + t * 16, levels), :] = forcing_ref[0, r, t].astype(F32)
    first, second = one_hot(devices * 8, code), one_hot(devices * 8, code + 4.0)
    lane = iota((records, LANES), 1)
    edges = jnp.zeros((records, LANES), F32)
    pair = []
    for k in range(count):
        t, level = divmod(k, levels)
        values = wide[pl.ds(t * 16 + level, records, stride=32), :]
        turned = pltpu.roll(values, (6 * k + 3) % LANES, 1)
        edges = jnp.where((lane >= 6 * k) & (lane < 6 * k + 6), turned, edges)
        pair.append(values.astype(BF16))
        if k % 2 == 1:
            packed = dot(first, pair[0]) + dot(second, pair[1])
            out_ref[:, k // 2] = packed.astype(BF16).reshape(devices, 8, LANES)
            pair = []
    row_col = jnp.floor(block_col * 0.5) + 1.0
    mine = west_lane((records, LANES))
    data = lane < 6 * count
    from_west = jnp.where(data, jnp.where(mine, edges, 0.0), jnp.where(lane == 121, row_col, 0.0))
    from_east = jnp.where(data, jnp.where(mine, 0.0, edges), jnp.where(lane == 122, row_col, 0.0))
    header = jnp.where(lane == 120, block_col + 1.0, 0.0)
    last = (
        dot(first, header.astype(BF16))
        + dot(one_hot(devices * 8, to_east), from_west.astype(BF16))
        + dot(one_hot(devices * 8, to_west), from_east.astype(BF16))
    )
    out_ref[:, count // 2] = last.astype(BF16).reshape(devices, 8, LANES)


def pack_records(forcing, tile, block, live, devices, n_lon):
    records, levels, width = forcing.shape[1], forcing.shape[3], forcing.shape[4]
    return pl.pallas_call(
        functools.partial(pack_body, n_lon),
        name="pack_records",
        out_shape=jax.ShapeDtypeStruct((devices, levels + 1, 8, width), BF16),
        in_specs=[SMEM, VMEM, VMEM, VMEM],
        out_specs=VMEM,
        scratch_shapes=[pltpu.VMEM((records * 32, width), F32)],
        compiler_params=pltpu.CompilerParams(vmem_limit_bytes=48 << 20),
    )(live, tile, block, forcing)


def columns_body(adj_ref, east_ref, north_ref, mask_ref, out_ref, held):
    level, levels = pl.program_id(0), pl.num_programs(0)
    rows = adj_ref.shape[2]
    lane = iota((rows, LANES), 1)

    @pl.when(level == 0)
    def _():
        held[...] = jnp.zeros_like(held)

    def put(tile, place, field):
        ends = jnp.where(lane < 64, field[:, :LANES], field[:, LANES:])
        turned = pltpu.roll(ends, lax.rem(6 * place + 3, LANES), 1)
        inside = (lane >= 6 * place) & (lane < 6 * place + 6)
        held[tile] = jnp.where(inside, turned, held[tile])

    put(0, level, adj_ref[0, 0])
    put(0, levels + level, adj_ref[1, 0])
    put(1, level, east_ref[0])
    put(1, levels + level, north_ref[0])
    put(2, level, mask_ref[0].astype(F32))

    @pl.when(level == levels - 1)
    def _():
        for tile in range(3):
            out_ref[:, tile * LANES : (tile + 1) * LANES] = held[tile].astype(BF16)


def outer_columns(adj, east, north, mask):
    levels, rows, cells = east.shape
    field = pl.BlockSpec((1, rows, cells), lambda l: (l, 0, 0))
    return pl.pallas_call(
        columns_body,
        name="outer_columns",
        grid=(levels,),
        out_shape=jax.ShapeDtypeStruct((rows, 3 * LANES), BF16),
        in_specs=[pl.BlockSpec((2, 1, rows, cells), lambda l: (0, l, 0, 0)), field, field, field],
        out_specs=pl.BlockSpec((rows, 3 * LANES), lambda l: (0, 0)),
        scratch_shapes=[pltpu.VMEM((3, rows, LANES), F32)],
        compiler_params=pltpu.CompilerParams(vmem_limit_bytes=48 << 20),
    )(adj, east, north, mask)


def halo_tile(packed, place):
    lane = iota(packed.shape, 1)
    turned = pltpu.roll(packed, lax.rem(125 + 6 * LANES - 6 * place, LANES), 1)
    return jnp.where((lane < 3) | (lane >= 125), turned, 0.0)


def rows_body(west_ref, east_ref, ef_ref, nf_ref, mask_ref, halo_ref, low_ref, high_ref):
    levels, rows, cells = ef_ref.shape
    for tile in range(3):
        part = slice(tile * LANES, (tile + 1) * LANES)
        theirs = west_ref[:, part].astype(F32)
        merged = jnp.where(west_lane(theirs.shape), theirs, east_ref[:, part].astype(F32))
        halo_ref[:, part] = merged
    for out, base in ((low_ref, 0), (high_ref, rows - 8)):
        side = slice(base, base + 8)
        for level in range(levels):
            for f, (ref, tile, place) in enumerate(
                ((ef_ref, 1, level), (nf_ref, 1, levels + level), (mask_ref, 2, level))
            ):
                out[f, level, :, :cells] = ref[level, side, :].astype(BF16)
                packed = halo_ref[side, tile * LANES : (tile + 1) * LANES]
                out[f, level, :, cells:] = halo_tile(packed, place).astype(BF16)


def outer_rows(west, east, ef, nf, mask):
    levels, rows, cells = ef.shape
    edge = jax.ShapeDtypeStruct((3, levels, 8, cells + LANES), BF16)
    return pl.pallas_call(
        rows_body,
        name="outer_rows",
        out_shape=(jax.ShapeDtypeStruct((rows, 3 * LANES), F32), edge, edge),
        in_specs=[VMEM] * 5,
        out_specs=(VMEM,) * 3,
        compiler_params=pltpu.CompilerParams(vmem_limit_bytes=48 << 20),
    )(west, east, ef, nf, mask)


def place_body(arrived_ref, adj_ref, halo_ref, state_ref, low_ref, high_ref, hot, packed_ref):
    q = pl.program_id(0)
    devices = arrived_ref.shape[0]
    slots = devices * 8
    rows, cells = adj_ref.shape[1], adj_ref.shape[2]

    @pl.when(q == 0)
    def _():
        last = arrived_ref[:, arrived_ref.shape[1] - 1].astype(F32).reshape(slots, LANES)
        heads = last.T[120:128]
        later = pltpu.roll(heads, 4, 1)
        row = fiota((rows, slots), 0)
        for b, source in enumerate((heads, later)):
            for c in range(2):
                found = source[0:1] == 2.0 * row + (c + 1.0)
                hot[pl.ds((2 * b + c) * rows, rows), :] = jnp.where(found, 1.0, 0.0).astype(BF16)
        lane = iota((slots, LANES), 1)
        mine = west_lane((slots, LANES))
        from_west = jnp.where(mine & (lane < 120), last, 0.0).astype(BF16)
        from_east = jnp.where(mine | (lane >= 120), 0.0, last).astype(BF16)
        packed_ref[...] = (
            halo_ref[...]
            + dot(one_hot(rows, heads[1:2] - 1.0), from_west)
            + dot(one_hot(rows, heads[2:3] - 1.0), from_east)
        )

    values = arrived_ref[:, q].astype(F32).reshape(slots, LANES).astype(BF16)
    for b in range(2):
        for c in range(2):
            part = slice(c * LANES, (c + 1) * LANES)
            forced = dot(hot[pl.ds((2 * b + c) * rows, rows), :], values)
            state_ref[b, :, part] = adj_ref[b, :, part] + forced
        state_ref[b, :, cells:] = halo_tile(packed_ref[...], 2 * q + b)
        low_ref[b] = state_ref[b, 0:8, :].astype(BF16)
        high_ref[b] = state_ref[b, rows - 8 : rows, :].astype(BF16)


def place_records(arrived, adj, halo):
    slices, rows, cells = adj.shape
    devices = arrived.shape[0]
    wide = cells + LANES
    edge = jax.ShapeDtypeStruct((slices, 8, wide), BF16)
    edge_spec = pl.BlockSpec((2, 8, wide), lambda q: (q, 0, 0))
    return pl.pallas_call(
        place_body,
        name="place_records",
        grid=(slices // 2,),
        out_shape=(jax.ShapeDtypeStruct((slices, rows, wide), F32), edge, edge),
        in_specs=[
            pl.BlockSpec(arrived.shape, lambda q: (0, 0, 0, 0)),
            pl.BlockSpec((2, rows, cells), lambda q: (q, 0, 0)),
            pl.BlockSpec((rows, LANES), lambda q: (0, 0)),
        ],
        out_specs=(pl.BlockSpec((2, rows, wide), lambda q: (q, 0, 0)), edge_spec, edge_spec),
        scratch_shapes=[
            pltpu.VMEM((4 * rows, devices * 8), BF16),
            pltpu.VMEM((rows, LANES), F32),
        ],
        compiler_params=pltpu.CompilerParams(vmem_limit_bytes=48 << 20),
    )(arrived, adj, halo)


def steps_body(
    limit_ref,
    spread_ref,
    state_ref,
    state_low_ref,
    state_high_ref,
    ef_ref,
    nf_ref,
    mask_ref,
    halo_ref,
    low_ref,
    high_ref,
    out_ref,
    flow,
    ocean,
    coef,
    cells_a,
    cells_b,
):
    level, levels = pl.program_id(0), pl.num_programs(0)
    rows, width = ef_ref.shape[1], ef_ref.shape[2]
    tiles = 3
    tall = rows + 16
    inner = slice(16, 16 + rows)

    def gather(dest, f, ref, tile, place):
        for x in range(tiles):
            part = slice(x * LANES, (x + 1) * LANES)
            dest[x, 8:16] = low_ref[f, 0, :, part].astype(F32)
            dest[x, 16 + rows : 24 + rows] = high_ref[f, 0, :, part].astype(F32)
            if x < 2:
                dest[x, inner] = ref[0, :, part].astype(F32)
            else:
                packed = halo_ref[:, tile * LANES : (tile + 1) * LANES]
                dest[x, inner] = halo_tile(packed, place)

    gather(flow.at[0], 0, ef_ref, 1, level)
    gather(flow.at[1], 1, nf_ref, 1, levels + level)
    gather(ocean, 2, mask_ref, 2, level)

    lane = iota((8, LANES), 1)
    sub = iota((8, LANES), 0)

    def from_west(values, x):
        return jnp.where(lane == 0, pltpu.roll(values[(x + 2) % tiles], 1, 1), pltpu.roll(values[x], 1, 1))

    def neighbours(values):
        right = [pltpu.roll(v, LANES - 1, 1) for v in values]
        left = [pltpu.roll(v, 1, 1) for v in values]
        east = [jnp.where(lane == LANES - 1, right[(x + 1) % tiles], right[x]) for x in range(tiles)]
        west = [jnp.where(lane == 0, left[(x + 2) % tiles], left[x]) for x in range(tiles)]
        return east, west

    first_row, last_row = limit_ref[0], limit_ref[1]

    def one(t, carry):
        k = spread_ref[t, level]
        for i in range(1, 2 + tall // 8 - 1):
            at = slice(8 * i, 8 * i + 8)
            place = sub + (8 * i - 16) + first_row
            opened = jnp.where((place >= 0) & (place < last_row), k, 0.0)
            opened_s = jnp.where((place >= 1) & (place <= last_row), k, 0.0)
            unit_s = jnp.where((place >= 1) & (place <= last_row), 1.0, 0.0)
            unit = jnp.where((place >= 0) & (place < last_row), 1.0, 0.0)
            minus = [jnp.minimum(flow[0, x, at], 0.0) for x in range(tiles)]
            for x in range(tiles):
                ce = jnp.maximum(flow[0, x, at], 0.0) + k
                cw = k - from_west(minus, x)
                cn = jnp.maximum(flow[1, x, at], 0.0) * unit + opened
                south = flow[1, x, 8 * i - 1 : 8 * i + 7]
                cs = opened_s - jnp.minimum(south, 0.0) * unit_s
                coef[0, x, at] = 1.0 - ce - cw - cn - cs
                coef[1, x, at] = ce
                coef[2, x, at] = cw
                coef[3, x, at] = cn
                coef[4, x, at] = cs
        for x in range(tiles):
            part = slice(x * LANES, (x + 1) * LANES)
            cells_a[x, 8:16] = state_low_ref[t, 0, :, part].astype(F32) * ocean[x, 8:16]
            cells_a[x, inner] = state_ref[t, 0, :, part] * ocean[x, inner]
            after = slice(16 + rows, 24 + rows)
            cells_a[x, after] = state_high_ref[t, 0, :, part].astype(F32) * ocean[x, after]
        source, dest = cells_a, cells_b
        for step in range(STEPS):
            last = step == STEPS - 1
            edge = 1 if last else 0
            for i in range(1 + edge, 1 + tall // 8 - edge):
                at = slice(8 * i, 8 * i + 8)
                here = [source[x, at] for x in range(tiles)]
                east, west = neighbours(here)
                for x in range(2 if last else tiles):
                    north = source[x, 8 * i + 1 : 8 * i + 9]
                    south = source[x, 8 * i - 1 : 8 * i + 7]
                    total = (
                        coef[0, x, at] * here[x]
                        + coef[1, x, at] * east[x]
                        + coef[2, x, at] * west[x]
                        + coef[3, x, at] * north
                        + coef[4, x, at] * south
                    )
                    if last:
                        part = slice(x * LANES, (x + 1) * LANES)
                        out_ref[t, 0, 8 * i - 16 : 8 * i - 8, part] = total
                    else:
                        dest[x, at] = total * ocean[x, at]
            source, dest = dest, source
        return carry

    @pl.when(level == 0)
    def _():
        for ref in (cells_a, cells_b, flow.at[0], flow.at[1]):
            for x in range(tiles):
                ref[x, 0:8] = jnp.zeros((8, LANES), F32)
                ref[x, tall + 8 : tall + 16] = jnp.zeros((8, LANES), F32)

    lax.fori_loop(0, 2, one, 0)


def run_steps(limit, spread, state, state_low, state_high, ef, nf, mask, halo, low, high):
    levels, rows, width = ef.shape
    wide = width + LANES
    field = pl.BlockSpec((1, rows, width), lambda l: (l, 0, 0))
    per_level = lambda lead, height, span: pl.BlockSpec((lead, 1, height, span), lambda l: (0, l, 0, 0))
    tall = rows + 32
    return pl.pallas_call(
        steps_body,
        name="three_steps",
        grid=(levels,),
        out_shape=jax.ShapeDtypeStruct((2, levels, rows, width), F32),
        in_specs=[
            SMEM,
            SMEM,
            per_level(2, rows, wide),
            per_level(2, 8, wide),
            per_level(2, 8, wide),
            field,
            field,
            field,
            pl.BlockSpec(halo.shape, lambda l: (0, 0)),
            per_level(3, 8, wide),
            per_level(3, 8, wide),
        ],
        out_specs=per_level(2, rows, width),
        scratch_shapes=[
            pltpu.VMEM((2, 3, tall, LANES), F32),
            pltpu.VMEM((3, tall, LANES), F32),
            pltpu.VMEM((5, 3, tall, LANES), F32),
            pltpu.VMEM((3, tall, LANES), F32),
            pltpu.VMEM((3, tall, LANES), F32),
        ],
        compiler_params=pltpu.CompilerParams(vmem_limit_bytes=48 << 20),
    )(limit, spread, state, state_low, state_high, ef, nf, mask, halo, low, high)


def around(block, axis, distance):
    count = lax.axis_size(axis)
    return lax.ppermute(block, axis, [(i, (i + distance) % count) for i in range(count)])


def along(block, axis, distance):
    count = lax.axis_size(axis)
    route = [(i, i + distance) for i in range(count) if 0 <= i + distance < count]
    return lax.ppermute(block, axis, route)


def per_device(
    adjoint_in,
    east_flow,
    north_flow,
    diffusivity,
    land_mask,
    forcing,
    obs_tile,
    obs_block,
    obs_live,
):
    n_lat, n_lon = lax.axis_size("lat"), lax.axis_size("lon")
    levels, rows, cells = east_flow.shape
    slices = 2 * levels
    packed = pack_records(forcing, obs_tile, obs_block, obs_live, n_lat * n_lon, n_lon)
    arrived = lax.all_to_all(packed, ("lat", "lon"), split_axis=0, concat_axis=0, tiled=True)
    columns = outer_columns(adjoint_in, east_flow, north_flow, land_mask)
    west = around(columns, "lon", 1)
    east = around(columns, "lon", -1)
    halo, low, high = outer_rows(west, east, east_flow, north_flow, land_mask)
    below = along(high, "lat", 1)
    above = along(low, "lat", -1)
    state, state_low, state_high = place_records(
        arrived, adjoint_in.reshape(slices, rows, cells), halo
    )
    state_below = along(state_high, "lat", 1)
    state_above = along(state_low, "lat", -1)
    wide = cells + LANES
    first = lax.axis_index("lat") * rows
    limit = jnp.stack([first, n_lat * rows - 1]).astype(jnp.int32)
    return run_steps(
        limit,
        diffusivity,
        state.reshape(2, levels, rows, wide),
        state_below.reshape(2, levels, 8, wide),
        state_above.reshape(2, levels, 8, wide),
        east_flow,
        north_flow,
        land_mask,
        halo,
        below,
        above,
    )


def solution(mesh):
    in_specs = (
        P(None, None, "lat", "lon"),
        P(None, "lat", "lon"),
        P(None, "lat", "lon"),
        P(),
        P(None, "lat", "lon"),
        P(("lat", "lon"), None, None, None, None),
        P(("lat", "lon"), None),
        P(("lat", "lon"), None),
        P(("lat", "lon")),
    )
    out_specs = P(None, None, "lat", "lon")
    return jax.shard_map(
        per_device, mesh=mesh, in_specs=in_specs, out_specs=out_specs, check_vma=False
    )
```

```python
import functools

import jax
import jax.numpy as jnp
from jax import lax
from jax.experimental import pallas as pl
from jax.experimental.pallas import tpu as pltpu
from jax.sharding import PartitionSpec as P

STEPS = 3
LANES = 128
F32 = jnp.float32
BF16 = jnp.bfloat16
HBM = pl.BlockSpec(memory_space=pltpu.HBM)
VMEM = pl.BlockSpec(memory_space=pltpu.VMEM)
SMEM = pl.BlockSpec(memory_space=pltpu.SMEM)


def iota(shape, dim):
    return lax.broadcasted_iota(jnp.int32, shape, dim)


def fiota(shape, dim):
    return iota(shape, dim).astype(F32)


def west_lane(shape):
    lane = fiota(shape, 1)
    return lane - 6.0 * jnp.floor((lane + 0.5) / 6.0) < 3.0


def one_hot(rows, code):
    shape = (rows, code.shape[1])
    return jnp.where(fiota(shape, 0) == code, 1.0, 0.0).astype(BF16)


def dot(a, b):
    return jnp.dot(a, b, preferred_element_type=F32)


def pack_body(
    n_lon, live_ref, tile_in, block_in, forcing_in, out_hbm,
    tile_ref, block_ref, forcing_ref, out_ref, wide, sems, out_sems,
):
    records, levels = forcing_ref.shape[1], forcing_ref.shape[2]
    count = 2 * levels
    devices = out_ref.shape[0]
    moves = [
        pltpu.make_async_copy(source, dest, sems.at[i])
        for i, (source, dest) in enumerate(
            (
                (tile_in, tile_ref),
                (block_in, block_ref),
                (forcing_in, forcing_ref),
            )
        )
    ]
    for move in moves:
        move.start()
    for move in moves[:2]:
        move.wait()
    tile = tile_ref[...].astype(F32)
    block = block_ref[...].astype(F32)
    square = (records, records)
    low, high = iota(square, 0), iota(square, 1)
    tile_col = jnp.sum(jnp.where(low == high, tile, 0.0), axis=1, keepdims=True)
    block_col = jnp.sum(jnp.where(low == high, block, 0.0), axis=1, keepdims=True)
    earlier = jnp.where((tile_col == tile) & (low < high), 1.0, 0.0)
    rank = jnp.sum(earlier, axis=0, keepdims=True)
    live = iota((1, records), 1) < live_ref[0]
    band = jnp.floor((tile + 0.5) / n_lon) * n_lon
    column = tile - band
    east = band + jnp.where(column == n_lon - 1, 0.0, column + 1.0)
    west = band + jnp.where(column == 0.0, n_lon - 1.0, column - 1.0)
    half = block - 2.0 * jnp.floor(block * 0.5)
    code = jnp.where(live, tile * 8.0 + rank, -8.0)
    to_east = jnp.where(live & (half == 1.0), east * 8.0 + rank, -8.0)
    to_west = jnp.where(live & (half == 0.0), west * 8.0 + rank, -8.0)
    moves[2].wait()

    def widen(r, carry):
        for level in range(levels):
            wide[pl.ds(r * count + 2 * level, 2), :] = forcing_ref[0, r, level].astype(F32)
        return carry

    lax.fori_loop(0, records, widen, 0, unroll=4)
    sent = []

    def send(q, values):
        out_ref[:, q] = values.astype(BF16).reshape(devices, 8, LANES)
        copy = pltpu.make_async_copy(out_ref.at[:, q], out_hbm.at[:, q], out_sems.at[q])
        copy.start()
        sent.append(copy)

    first, second = one_hot(devices * 8, code), one_hot(devices * 8, code + 4.0)
    lane = iota((records, LANES), 1)
    edges = jnp.zeros((records, LANES), F32)
    pair = []
    for place in range(count):
        level, t = divmod(place, 2)
        k = t * levels + level
        values = wide[pl.ds(place, records, stride=count), :]
        turned = pltpu.roll(values, (6 * k + 3) % LANES, 1)
        edges = jnp.where((lane >= 6 * k) & (lane < 6 * k + 6), turned, edges)
        pair.append(values.astype(BF16))
        if t == 1:
            packed = dot(first, pair[0]) + dot(second, pair[1])
            send(level, packed)
            pair = []
    row_col = jnp.floor(block_col * 0.5) + 1.0
    mine = west_lane((records, LANES))
    data = lane < 6 * count
    from_west = jnp.where(data, jnp.where(mine, edges, 0.0), jnp.where(lane == 121, row_col, 0.0))
    from_east = jnp.where(data, jnp.where(mine, 0.0, edges), jnp.where(lane == 122, row_col, 0.0))
    header = jnp.where(lane == 120, block_col + 1.0, 0.0)
    last = (
        dot(first, header.astype(BF16))
        + dot(one_hot(devices * 8, to_east), from_west.astype(BF16))
        + dot(one_hot(devices * 8, to_west), from_east.astype(BF16))
    )
    send(count // 2, last)
    for copy in sent:
        copy.wait()


def pack_records(forcing, tile, block, live, devices, n_lon):
    records, levels, width = forcing.shape[1], forcing.shape[2], forcing.shape[4]
    out = (devices, levels + 1, 8, width)
    return pl.pallas_call(
        functools.partial(pack_body, n_lon),
        name="pack_records",
        out_shape=pltpu.HBM(out, BF16),
        in_specs=[SMEM] + [HBM] * 3,
        out_specs=HBM,
        scratch_shapes=[
            pltpu.VMEM(tile.shape, jnp.int32),
            pltpu.VMEM(block.shape, jnp.int32),
            pltpu.VMEM(forcing.shape, BF16),
            pltpu.VMEM(out, BF16),
            pltpu.VMEM((records * levels * 2, width), F32),
            pltpu.SemaphoreType.DMA((3,)),
            pltpu.SemaphoreType.DMA((levels + 1,)),
        ],
        compiler_params=pltpu.CompilerParams(vmem_limit_bytes=24 << 20),
    )(live, *map(hbm, (tile, block, forcing)))


STRIPS = 3


def strip_of(k):
    return k // 7, 18 * lax.rem(k, 7) if not isinstance(k, int) else 18 * (k % 7)


def turn(values, shift):
    if isinstance(shift, int):
        return pltpu.roll(values, shift % LANES, 1)
    return pltpu.roll(values, lax.rem(shift + 4 * LANES, LANES), 1)


def hbm(x):
    return pltpu.with_memory_space_constraint(x, pltpu.HBM)


def between(lane, low, high):
    return (lane >= low) & (lane < high)


def columns_body(
    adj_hbm, ef_hbm, nf_hbm, mask_hbm, out_ref, ocean_ref, adj_ref, flow_ref, mask, held, sems
):
    levels, rows = mask.shape[0], mask.shape[1]

    def moves(level):
        pairs = [(mask_hbm.at[level], mask.at[level])]
        pairs += [(adj_hbm.at[t, level], adj_ref.at[t, level]) for t in range(2)]
        pairs += [
            (
                source.at[level, :, pl.ds(x * LANES, LANES)],
                flow_ref.at[level, f, x],
            )
            for f, source in enumerate((ef_hbm, nf_hbm))
            for x in range(2)
        ]
        return [
            pltpu.make_async_copy(source, dest, sems.at[i, level])
            for i, (source, dest) in enumerate(pairs)
        ]

    for level in range(levels):
        for copy in moves(level):
            copy.start()
    lane = iota((rows, LANES), 1)
    held[...] = jnp.zeros_like(held)

    def put(tile, place, first, second):
        ends = jnp.where(lane < 64, first, second)
        inside = between(lane, 6 * place, 6 * place + 6)
        held[tile] = jnp.where(inside, turn(ends, 6 * place + 3), held[tile])

    def one(level, carry):
        for copy in moves(level):
            copy.wait()
        for x in range(2):
            ocean_ref[level, x] = mask[level, :, x * LANES : (x + 1) * LANES].astype(F32)
        for t in range(2):
            put(0, t * levels + level, adj_ref[t, level, :, :LANES], adj_ref[t, level, :, LANES:])
        put(1, level, flow_ref[level, 0, 0], flow_ref[level, 0, 1])
        put(1, levels + level, flow_ref[level, 1, 0], flow_ref[level, 1, 1])
        put(2, level, ocean_ref[level, 0], ocean_ref[level, 1])
        return carry

    lax.fori_loop(0, levels, one, 0)
    for tile in range(3):
        out_ref[:, tile * LANES : (tile + 1) * LANES] = held[tile].astype(BF16)


def outer_columns(adj, ef, nf, mask):
    levels, rows, cells = ef.shape
    return pl.pallas_call(
        columns_body,
        name="outer_columns",
        out_shape=(
            jax.ShapeDtypeStruct((rows, 3 * LANES), BF16),
            jax.ShapeDtypeStruct((levels, 2, rows, LANES), F32),
        ),
        in_specs=[HBM] * 4,
        out_specs=(VMEM,) * 2,
        scratch_shapes=[
            pltpu.VMEM(adj.shape, F32),
            pltpu.VMEM((levels, 2, 2, rows, LANES), F32),
            pltpu.VMEM(mask.shape, jnp.int32),
            pltpu.VMEM((3, rows, LANES), F32),
            pltpu.SemaphoreType.DMA((7, levels)),
        ],
        compiler_params=pltpu.CompilerParams(vmem_limit_bytes=24 << 20),
    )(*map(hbm, (adj, ef, nf, mask)))


def own_body(ef_hbm, nf_hbm, ocean_ref, strips, spread_ref, flow_ref, sems):
    levels, rows = ocean_ref.shape[0], ocean_ref.shape[2]

    def moves(level):
        return [
            pltpu.make_async_copy(
                source.at[level, :, pl.ds(x * LANES, LANES)],
                flow_ref.at[level, f, x],
                sems.at[2 * f + x, level],
            )
            for f, source in enumerate((ef_hbm, nf_hbm))
            for x in range(2)
        ]

    for level in range(levels):
        for copy in moves(level):
            copy.start()
    square = (LANES, LANES)
    source, target = fiota(square, 0), fiota(square, 1)
    order = jnp.floor((target + 0.5) / 18.0)
    offset = target - 18.0 * order
    inner = jnp.where(offset < 3.0, offset, offset - 12.0)
    used = ((offset < 3.0) | (offset >= 15.0)) & (order < 7.0)
    for tile in range(STRIPS):
        k = order + 7.0 * tile
        level = jnp.where(k < levels, k, k - levels)
        live = used & (k < 2.0 * levels)
        for m, place in enumerate((k, level, level + levels)):
            hit = live & (source == 6.0 * place + inner)
            spread_ref[m, :, tile * LANES : (tile + 1) * LANES] = jnp.where(hit, 1.0, 0.0).astype(BF16)
    strips[...] = jnp.zeros_like(strips)
    lane = iota((rows, LANES), 1)

    def one(level, carry):
        for copy in moves(level):
            copy.wait()
        for f, ref in enumerate((flow_ref.at[level, 0], flow_ref.at[level, 1], ocean_ref.at[level])):
            own = jnp.where(lane < 9, turn(ref[0], 3), turn(ref[1], 15))
            for t in range(2):
                tile, first = strip_of(t * levels + level)
                keep = between(lane, first + 3, first + 15)
                strips[f, tile] = jnp.where(keep, turn(own, first), strips[f, tile])
        return carry

    lax.fori_loop(0, levels, one, 0)


def own_strips(ef, nf, ocean):
    levels, rows = ef.shape[0], ef.shape[1]
    return pl.pallas_call(
        own_body,
        name="own_strips",
        out_shape=(
            jax.ShapeDtypeStruct((3, STRIPS, rows, LANES), F32),
            jax.ShapeDtypeStruct((3, LANES, STRIPS * LANES), BF16),
        ),
        in_specs=[HBM, HBM, VMEM],
        out_specs=(VMEM, VMEM),
        scratch_shapes=[
            pltpu.VMEM((levels, 2, 2, rows, LANES), F32),
            pltpu.SemaphoreType.DMA((4, levels)),
        ],
        cost_estimate=pl.CostEstimate(flops=10**8, bytes_accessed=10**7, transcendentals=0),
        compiler_params=pltpu.CompilerParams(vmem_limit_bytes=24 << 20),
    )(hbm(ef), hbm(nf), ocean)


def edges_body(
    west, east, ef_hbm, nf_hbm, ocean_ref, own_ref, spread_ref,
    strips, adj, low_out, high_out, low, high, ends, sems,
):
    levels, rows = ocean_ref.shape[0], ocean_ref.shape[2]
    copies = [
        pltpu.make_async_copy(
            source.at[:, pl.ds(base, 8), :], ends.at[side, f], sems.at[side, f]
        )
        for side, base in ((0, 0), (1, rows - 8))
        for f, source in enumerate((ef_hbm, nf_hbm))
    ]
    for copy in copies:
        copy.start()
    low[...] = jnp.zeros_like(low)
    high[...] = jnp.zeros_like(high)

    def halo(tile, m):
        part = slice(tile * LANES, (tile + 1) * LANES)
        theirs, ours = west[:, part].astype(F32), east[:, part].astype(F32)
        merged = jnp.where(west_lane(theirs.shape), theirs, ours).astype(BF16)
        return dot(merged, spread_ref[m])

    halos = halo(0, 0)
    for tile in range(STRIPS):
        adj[tile] = halos[:, tile * LANES : (tile + 1) * LANES]
    for f, (source, m) in enumerate(((1, 1), (1, 2), (2, 1))):
        halos = halo(source, m)
        for tile in range(STRIPS):
            strips[f, tile] = own_ref[f, tile] + halos[:, tile * LANES : (tile + 1) * LANES]
    for copy in copies:
        copy.wait()
    for side, (out, first, near) in enumerate(((low, 0, 0), (high, rows - 3, 5))):
        strip_at = slice(first, first + 3)
        for f in range(3):
            here = slice(3 * f, 3 * f + 3)
            for level in range(levels):
                if f < 2:
                    out[level, here, :] = ends[side, f, level, near : near + 3, :]
                else:
                    out[level, here, :LANES] = ocean_ref[level, 0, strip_at]
                    out[level, here, LANES:] = ocean_ref[level, 1, strip_at]
            out[levels, here, :LANES] = strips[f, 0, strip_at, :]
            out[levels, here, LANES:] = strips[f, 1, strip_at, :]
            out[levels + 1, here, :LANES] = strips[f, 2, strip_at, :]
    low_out[...] = low[...].astype(BF16)
    high_out[...] = high[...].astype(BF16)


def outer_rows(west, east, ef, nf, ocean, own, spread):
    levels = ef.shape[0]
    edge = (levels + 2, 16, 2 * LANES)
    return pl.pallas_call(
        edges_body,
        name="outer_rows",
        out_shape=(
            jax.ShapeDtypeStruct(own.shape, F32),
            jax.ShapeDtypeStruct(own.shape[1:], F32),
            jax.ShapeDtypeStruct(edge, BF16),
            jax.ShapeDtypeStruct(edge, BF16),
        ),
        in_specs=[VMEM, VMEM, HBM, HBM] + [VMEM] * 3,
        out_specs=(VMEM,) * 4,
        scratch_shapes=[
            pltpu.VMEM(edge, F32),
            pltpu.VMEM(edge, F32),
            pltpu.VMEM((2, 2, levels, 8, 2 * LANES), F32),
            pltpu.SemaphoreType.DMA((2, 2)),
        ],
        compiler_params=pltpu.CompilerParams(vmem_limit_bytes=24 << 20),
    )(west, east, hbm(ef), hbm(nf), ocean, own, spread)


def place_body(
    odd_ref,
    arrived_ref,
    adj_hbm,
    ocean_ref,
    strip_ref,
    fields_ref,
    spread_ref,
    state_ref,
    out_strip_ref,
    swap_a_ref,
    swap_b_ref,
    adj_ref,
    hot,
    low,
    high,
    sems,
):
    devices = arrived_ref.shape[0]
    slots = devices * 8
    levels, rows = adj_ref.shape[1], adj_ref.shape[2]

    def arrival(level):
        return pltpu.make_async_copy(adj_hbm.at[:, level], adj_ref.at[:, level], sems.at[level])

    for level in range(levels):
        arrival(level).start()
    last = arrived_ref[:, levels].astype(F32).reshape(slots, LANES)
    heads = last.T[120:128]
    later = pltpu.roll(heads, 4, 1)
    row = fiota((rows, slots), 0)
    for b, source in enumerate((heads, later)):
        for c in range(2):
            found = source[0:1] == 2.0 * row + (c + 1.0)
            hot[pl.ds((2 * b + c) * rows, rows), :] = jnp.where(found, 1.0, 0.0).astype(BF16)
    lane = iota((slots, LANES), 1)
    mine = west_lane((slots, LANES))
    from_west = jnp.where(mine & (lane < 120), last, 0.0).astype(BF16)
    from_east = jnp.where(mine | (lane >= 120), 0.0, last).astype(BF16)
    spread = spread_ref[0]
    strips = dot(one_hot(rows, heads[1:2] - 1.0), dot(from_west, spread).astype(BF16)) + dot(
        one_hot(rows, heads[2:3] - 1.0), dot(from_east, spread).astype(BF16)
    )
    for tile in range(STRIPS):
        out_strip_ref[tile] = strip_ref[tile] + strips[:, tile * LANES : (tile + 1) * LANES]
    low[...] = jnp.zeros_like(low)
    high[...] = jnp.zeros_like(high)
    wide = iota((rows, LANES), 1)

    def one(level, carry):
        values = arrived_ref[:, level].astype(F32).reshape(slots, LANES).astype(BF16)
        arrival(level).wait()
        for t in range(2):
            k = t * levels + level
            tile, first = strip_of(k)
            ends = []
            for c in range(2):
                part = slice(c * LANES, (c + 1) * LANES)
                forced = dot(hot[pl.ds((2 * t + c) * rows, rows), :], values)
                total = adj_ref[t, level, :, part] + forced
                ends.append(total)
                masked = total * ocean_ref[level, c]
                state_ref[k, c] = masked
                low[level, 3 * t : 3 * t + 3, part] = masked[0:3]
                high[level, 3 * t : 3 * t + 3, part] = masked[rows - 3 : rows]
            held = out_strip_ref[tile]
            held = jnp.where(between(wide, first + 3, first + 9), turn(ends[0], first + 3), held)
            out_strip_ref[tile] = jnp.where(
                between(wide, first + 9, first + 15), turn(ends[1], first + 15), held
            )
        return carry

    lax.fori_loop(0, levels, one, 0)
    for tile in range(STRIPS):
        out_strip_ref[tile] = out_strip_ref[tile] * fields_ref[2, tile]
    for out, side in ((low, slice(0, 3)), (high, slice(rows - 3, rows))):
        out[levels, 0:3, :LANES] = out_strip_ref[0, side, :]
        out[levels, 0:3, LANES:] = out_strip_ref[1, side, :]
        out[levels, 3:6, :LANES] = out_strip_ref[2, side, :]
    odd = odd_ref[0] == 1
    swap_a_ref[...] = jnp.where(odd, low[...], high[...]).astype(BF16)
    swap_b_ref[...] = jnp.where(odd, high[...], low[...]).astype(BF16)


def place_records(odd, arrived, adj, ocean, strip, fields, spread):
    levels, rows, cells = adj.shape[1:]
    devices = arrived.shape[0]
    edge = jax.ShapeDtypeStruct((levels + 1, 8, cells), BF16)
    return pl.pallas_call(
        place_body,
        name="place_records",
        out_shape=(
            jax.ShapeDtypeStruct((2 * levels, 2, rows, LANES), F32),
            jax.ShapeDtypeStruct((STRIPS, rows, LANES), F32),
            edge,
            edge,
        ),
        in_specs=[SMEM, VMEM, HBM] + [VMEM] * 4,
        out_specs=(VMEM,) * 4,
        scratch_shapes=[
            pltpu.VMEM(adj.shape, F32),
            pltpu.VMEM((4 * rows, devices * 8), BF16),
            pltpu.VMEM(edge.shape, F32),
            pltpu.VMEM(edge.shape, F32),
            pltpu.SemaphoreType.DMA((levels,)),
        ],
        compiler_params=pltpu.CompilerParams(vmem_limit_bytes=24 << 20),
    )(odd, arrived, hbm(adj), ocean, strip, fields, spread)


def steps_body(
    where_ref,
    spread_ref,
    state_ref,
    strip_ref,
    swap_a_ref,
    swap_b_ref,
    ef_hbm,
    nf_hbm,
    ocean_ref,
    fields_ref,
    low_ref,
    high_ref,
    out_ref,
    flow_all,
    ocean,
    strip_flow,
    strip_ocean,
    coef,
    cells_a,
    cells_b,
    cells_c,
    patch,
    below,
    above,
    rows_low,
    rows_high,
    done,
    sems,
    level_sems,
):
    levels, rows = ocean_ref.shape[0], ocean_ref.shape[2]

    def arrivals(level):
        return [
            pltpu.make_async_copy(
                source.at[level, :, pl.ds(x * LANES, LANES)],
                flow_all.at[level, f, x, pl.ds(16, rows), :],
                level_sems.at[2 * f + x, level],
            )
            for f, source in enumerate((ef_hbm, nf_hbm))
            for x in range(2)
        ]

    for level in range(levels):
        for copy in arrivals(level):
            copy.start()
    tall = rows + 16
    inner = slice(16, 16 + rows)
    before, after = slice(13, 16), slice(16 + rows, 19 + rows)
    at_start, at_end, odd = where_ref[0], where_ref[1], where_ref[2] == 1
    lane, sub = iota((8, LANES), 1), iota((8, LANES), 0)
    for ref in (strip_flow.at[0], strip_flow.at[1], strip_ocean):
        ref[0, 0:16] = jnp.zeros((16, LANES), F32)
        ref[0, 16 + rows : 32 + rows] = jnp.zeros((16, LANES), F32)
    for x in range(2):
        ocean[x, 0:16] = jnp.zeros((16, LANES), F32)
        ocean[x, 16 + rows : 32 + rows] = jnp.zeros((16, LANES), F32)
    for ref in (cells_a, cells_b, cells_c):
        for t in range(2):
            for x in range(2):
                ref[t, x, 0:16] = jnp.zeros((16, LANES), F32)
                ref[t, x, 16 + rows : 32 + rows] = jnp.zeros((16, LANES), F32)
    below[...] = jnp.where(odd, swap_a_ref[...].astype(F32), swap_b_ref[...].astype(F32))
    above[...] = jnp.where(odd, swap_b_ref[...].astype(F32), swap_a_ref[...].astype(F32))
    rows_low[...] = low_ref[...].astype(F32)
    rows_high[...] = high_ref[...].astype(F32)
    top = 8 + rows
    shut_s = (sub == 0) & (at_start == 1)
    shut_n = (sub == 7) & (at_end == 1)

    def close_top(ref):
        ref[top : top + 8] = jnp.where(shut_n, 0.0, ref[top : top + 8])

    def prepare(x, i, flow, here, turned):
        at = slice(8 * i, 8 * i + 8)
        ce = jnp.maximum(here, 0.0)
        cw = -jnp.minimum(turned, 0.0)
        cn = jnp.maximum(flow[1, x, at], 0.0)
        cs = -jnp.minimum(flow[1, x, 8 * i - 1 : 8 * i + 7], 0.0)
        coef[0, x, at] = ce
        coef[1, x, at] = cw
        coef[2, x, at] = cn
        coef[3, x, at] = cs
        coef[4, x, at] = 1.0 - ce - cw - cn - cs

    def around_k(i, k):
        total = 4.0 * k
        if i == 2:
            total = total - jnp.where(shut_s, k, 0.0)
        if i == 1 + rows // 8:
            total = total - jnp.where(shut_n, k, 0.0)
        return total

    def update(source, x, i, k, here, east, west):
        at = slice(8 * i, 8 * i + 8)
        north = source[x, 8 * i + 1 : 8 * i + 9]
        south = source[x, 8 * i - 1 : 8 * i + 7]
        return (
            (coef[4, x, at] - around_k(i, k)) * here
            + (coef[0, x, at] + k) * east
            + (coef[1, x, at] + k) * west
            + (coef[2, x, at] + k) * north
            + (coef[3, x, at] + k) * south
        )

    def tiles(step):
        edge = 1 if step == STEPS - 1 else 0
        return range(1 + edge, 1 + tall // 8 - edge)

    for tile in range(STRIPS):
        k = jnp.zeros((1, LANES), F32)
        for s in range(7):
            slice_id = 7 * tile + s
            if slice_id < 2 * levels:
                own = between(iota((1, LANES), 1), 18 * s, 18 * s + 18)
                k = jnp.where(own, spread_ref[slice_id // levels, slice_id % levels], k)
        block = levels + tile // 2
        part = slice((tile % 2) * LANES, (tile % 2 + 1) * LANES)
        for f, dest in enumerate((strip_flow.at[0, 0], strip_flow.at[1, 0], strip_ocean.at[0])):
            dest[before] = rows_low[block, 3 * f : 3 * f + 3, part]
            dest[inner] = fields_ref[f, tile]
            dest[after] = rows_high[block, 3 * f : 3 * f + 3, part]
        close_top(strip_flow.at[1, 0])
        for i in range(1, 1 + tall // 8):
            face = strip_flow[0, 0, 8 * i : 8 * i + 8]
            prepare(0, i, strip_flow, face, pltpu.roll(face, 1, 1))
        here = slice(3 * (tile // 2), 3 * (tile // 2) + 3)
        cells_a[0, 0, before] = below[levels, here, part]
        cells_a[0, 0, inner] = strip_ref[tile]
        cells_a[0, 0, after] = above[levels, here, part]
        source = cells_a.at[0]
        for step in range(STEPS):
            dest = (cells_b, cells_c, None)[step]
            for i in tiles(step):
                at = slice(8 * i, 8 * i + 8)
                value = source[0, at]
                total = update(
                    source, 0, i, k, value, pltpu.roll(value, LANES - 1, 1), pltpu.roll(value, 1, 1)
                )
                if dest is None:
                    patch[tile, 8 * i - 16 : 8 * i - 8] = total
                else:
                    dest[0, 0, at] = total * strip_ocean[0, at]
            source = dest.at[0] if dest is not None else None

    def copies(level, slot):
        return [
            pltpu.make_async_copy(done.at[slot, t], out_ref.at[t, level], sems.at[slot, t])
            for t in range(2)
        ]

    def one(level, carry):
        flow = flow_all.at[level]
        for copy in arrivals(level):
            copy.wait()
        for f in range(2):
            for x in range(2):
                flow[f, x, 0:16] = jnp.zeros((16, LANES), F32)
                flow[f, x, 16 + rows : 32 + rows] = jnp.zeros((16, LANES), F32)
        for x in range(2):
            part = slice(x * LANES, (x + 1) * LANES)
            ocean[x, inner] = ocean_ref[level, x]
            for f, dest in enumerate((flow.at[0, x], flow.at[1, x], ocean.at[x])):
                dest[before] = rows_low[level, 3 * f : 3 * f + 3, part]
                dest[after] = rows_high[level, 3 * f : 3 * f + 3, part]
            close_top(flow.at[1, x])
            for t in range(2):
                cells_a[t, x, before] = below[level, 3 * t : 3 * t + 3, part]
                cells_a[t, x, inner] = state_ref[t * levels + level, x]
                cells_a[t, x, after] = above[level, 3 * t : 3 * t + 3, part]
        for i in range(1, 1 + tall // 8):
            at = slice(8 * i, 8 * i + 8)
            faces = [flow[0, x, at] for x in range(2)]
            turned = [pltpu.roll(v, 1, 1) for v in faces]
            turned[1] = jnp.where(lane == 0, turned[0], turned[1])
            for x in range(2):
                prepare(x, i, flow, faces[x], turned[x])
        slot = lax.rem(level, 2)

        @pl.when(level >= 2)
        def _():
            for copy in copies(level - 2, slot):
                copy.wait()

        ks = [spread_ref[t, level] for t in range(2)]
        spots = [strip_of(t * levels + level) for t in range(2)]
        buffers = (cells_a, cells_b, cells_c)
        for step in range(STEPS):
            for i in tiles(step):
                at = slice(8 * i, 8 * i + 8)
                for t in range(2):
                    source = buffers[step].at[t]
                    here = [source[x, at] for x in range(2)]
                    right = [pltpu.roll(v, LANES - 1, 1) for v in here]
                    left = [pltpu.roll(v, 1, 1) for v in here]
                    east = [jnp.where(lane == LANES - 1, right[1], right[0]), right[1]]
                    west = [left[0], jnp.where(lane == 0, left[0], left[1])]
                    for x in range(2):
                        total = update(source, x, i, ks[t], here[x], east[x], west[x])
                        if step < STEPS - 1:
                            buffers[step + 1][t, x, at] = total * ocean[x, at]
                            continue
                        tile, first = spots[t]
                        shift, keep = (125 - first, lane < 3) if x == 0 else (113 - first, lane >= 125)
                        fixed = turn(patch[tile, 8 * i - 16 : 8 * i - 8], shift)
                        done[slot, t, 8 * i - 16 : 8 * i - 8, x * LANES : (x + 1) * LANES] = (
                            jnp.where(keep, fixed, total)
                        )
        for copy in copies(level, slot):
            copy.start()
        return carry

    lax.fori_loop(0, levels, one, 0)
    for level in (levels - 2, levels - 1):
        for copy in copies(level, level % 2):
            copy.wait()


def run_steps(where, spread, state, strip, swap_a, swap_b, ef, nf, ocean, fields, low, high):
    levels, rows = ocean.shape[0], ocean.shape[2]
    tall, width = rows + 32, 2 * LANES
    buffer = pltpu.VMEM((2, 2, tall, LANES), F32)
    return pl.pallas_call(
        steps_body,
        name="three_steps",
        out_shape=jax.ShapeDtypeStruct((2, levels, rows, width), F32),
        in_specs=[SMEM, SMEM] + [VMEM] * 4 + [HBM] * 2 + [VMEM] * 4,
        out_specs=HBM,
        scratch_shapes=[
            pltpu.VMEM((levels, 2, 2, tall, LANES), F32),
            pltpu.VMEM((2, tall, LANES), F32),
            pltpu.VMEM((2, 1, tall, LANES), F32),
            pltpu.VMEM((1, tall, LANES), F32),
            pltpu.VMEM((5, 2, tall, LANES), F32),
            buffer,
            buffer,
            buffer,
            pltpu.VMEM((STRIPS, rows, LANES), F32),
            pltpu.VMEM(swap_a.shape, F32),
            pltpu.VMEM(swap_a.shape, F32),
            pltpu.VMEM(low.shape, F32),
            pltpu.VMEM(low.shape, F32),
            pltpu.VMEM((2, 2, rows, width), F32),
            pltpu.SemaphoreType.DMA((2, 2)),
            pltpu.SemaphoreType.DMA((4, levels)),
        ],
        compiler_params=pltpu.CompilerParams(vmem_limit_bytes=24 << 20),
    )(where, spread, state, strip, swap_a, swap_b, hbm(ef), hbm(nf), ocean, fields, low, high)


def around(block, axis, distance):
    count = lax.axis_size(axis)
    return lax.ppermute(block, axis, [(i, (i + distance) % count) for i in range(count)])


def along(block, axis, distance):
    count = lax.axis_size(axis)
    route = [(i, i + distance) for i in range(count) if 0 <= i + distance < count]
    return lax.ppermute(block, axis, route)


def swapped(block, axis, start):
    count = lax.axis_size(axis)
    lower = range(start, count - 1, 2)
    return lax.ppermute(block, axis, [(i, i + 1) for i in lower] + [(i + 1, i) for i in lower])


def per_device(
    adjoint_in,
    east_flow,
    north_flow,
    diffusivity,
    land_mask,
    forcing,
    obs_tile,
    obs_block,
    obs_live,
):
    n_lat, n_lon = lax.axis_size("lat"), lax.axis_size("lon")
    lat = lax.axis_index("lat")
    odd = lat % 2
    where = jnp.stack([lat == 0, lat == n_lat - 1, odd == 1]).astype(jnp.int32)
    packed = pack_records(
        forcing.transpose(0, 1, 3, 2, 4), obs_tile, obs_block, obs_live, n_lat * n_lon, n_lon
    )
    arrived = lax.all_to_all(packed, ("lat", "lon"), split_axis=0, concat_axis=0, tiled=True)
    columns, ocean = outer_columns(adjoint_in, east_flow, north_flow, land_mask)
    west = around(columns, "lon", 1)
    east = around(columns, "lon", -1)
    own, spread = own_strips(east_flow, north_flow, ocean)
    fields, adj_strip, low, high = outer_rows(
        west, east, east_flow, north_flow, ocean, own, spread
    )
    below = along(high, "lat", 1)
    above = along(low, "lat", -1)
    state, strip, swap_a, swap_b = place_records(
        odd.reshape(1).astype(jnp.int32), arrived, adjoint_in, ocean, adj_strip, fields, spread
    )
    swap_a = swapped(swap_a, "lat", 0)
    swap_b = swapped(swap_b, "lat", 1)
    return run_steps(
        where,
        diffusivity,
        state,
        strip,
        swap_a,
        swap_b,
        east_flow,
        north_flow,
        ocean,
        fields,
        below,
        above,
    )


def solution(mesh):
    in_specs = (
        P(None, None, "lat", "lon"),
        P(None, "lat", "lon"),
        P(None, "lat", "lon"),
        P(),
        P(None, "lat", "lon"),
        P(("lat", "lon"), None, None, None, None),
        P(("lat", "lon"), None),
        P(("lat", "lon"), None),
        P(("lat", "lon")),
    )
    out_specs = P(None, None, "lat", "lon")
    return jax.shard_map(
        per_device, mesh=mesh, in_specs=in_specs, out_specs=out_specs, check_vma=False
    )
```

```python
import functools

import jax
import jax.numpy as jnp
from jax import lax
from jax.experimental import pallas as pl
from jax.experimental.pallas import tpu as pltpu
from jax.sharding import PartitionSpec as P

STEPS = 3
LANES = 128
KEPT = 9
F32 = jnp.float32
BF16 = jnp.bfloat16
HBM = pl.BlockSpec(memory_space=pltpu.HBM)
VMEM = pl.BlockSpec(memory_space=pltpu.VMEM)
SMEM = pl.BlockSpec(memory_space=pltpu.SMEM)


def iota(shape, dim):
    return lax.broadcasted_iota(jnp.int32, shape, dim)


def fiota(shape, dim):
    return iota(shape, dim).astype(F32)


def west_lane(shape):
    lane = fiota(shape, 1)
    return lane - 6.0 * jnp.floor((lane + 0.5) / 6.0) < 3.0


def one_hot(rows, code):
    shape = (rows, code.shape[1])
    return jnp.where(fiota(shape, 0) == code, 1.0, 0.0).astype(BF16)


def dot(a, b):
    return jnp.dot(a, b, preferred_element_type=F32)


def pack_body(
    n_lon, live_ref, tile_in, block_in, forcing_in, out_hbm,
    tile_ref, block_ref, forcing_ref, out_ref, wide, sems, out_sems,
):
    records, devices = tile_ref.shape[1], out_ref.shape[0]
    count = forcing_ref.shape[0] // records
    levels = count // 2
    moves = [
        pltpu.make_async_copy(source, dest, sems.at[i])
        for i, (source, dest) in enumerate(
            (
                (tile_in, tile_ref),
                (block_in, block_ref),
                (forcing_in, forcing_ref),
            )
        )
    ]
    for move in moves:
        move.start()
    for move in moves[:2]:
        move.wait()
    tile = tile_ref[...].astype(F32)
    block = block_ref[...].astype(F32)
    square = (records, records)
    low, high = iota(square, 0), iota(square, 1)
    tile_col = jnp.sum(jnp.where(low == high, tile, 0.0), axis=1, keepdims=True)
    block_col = jnp.sum(jnp.where(low == high, block, 0.0), axis=1, keepdims=True)
    earlier = jnp.where((tile_col == tile) & (low < high), 1.0, 0.0)
    rank = jnp.sum(earlier, axis=0, keepdims=True)
    live = iota((1, records), 1) < live_ref[0]
    band = jnp.floor((tile + 0.5) / n_lon) * n_lon
    column = tile - band
    east = band + jnp.where(column == n_lon - 1, 0.0, column + 1.0)
    west = band + jnp.where(column == 0.0, n_lon - 1.0, column - 1.0)
    half = block - 2.0 * jnp.floor(block * 0.5)
    code = jnp.where(live, tile * 8.0 + rank, -8.0)
    to_east = jnp.where(live & (half == 1.0), east * 8.0 + rank, -8.0)
    to_west = jnp.where(live & (half == 0.0), west * 8.0 + rank, -8.0)
    moves[2].wait()
    wide[...] = forcing_ref[...].astype(F32)
    sent = []

    def send(q, values):
        out_ref[:, q] = values.astype(BF16).reshape(devices, 8, LANES)
        copy = pltpu.make_async_copy(out_ref.at[:, q], out_hbm.at[:, q], out_sems.at[q])
        copy.start()
        sent.append(copy)

    first, second = one_hot(devices * 8, code), one_hot(devices * 8, code + 4.0)
    lane = iota((records, LANES), 1)
    edges = jnp.zeros((records, LANES), F32)
    pair = []
    for place in range(count):
        level, t = divmod(place, 2)
        k = t * levels + level
        values = wide[pl.ds(place, records, stride=count), :]
        turned = pltpu.roll(values, (6 * k + 3) % LANES, 1)
        edges = jnp.where((lane >= 6 * k) & (lane < 6 * k + 6), turned, edges)
        pair.append(values.astype(BF16))
        if t == 1:
            packed = dot(first, pair[0]) + dot(second, pair[1])
            send(level, packed)
            pair = []
    row_col = jnp.floor(block_col * 0.5) + 1.0
    mine = west_lane((records, LANES))
    data = lane < 6 * count
    from_west = jnp.where(data, jnp.where(mine, edges, 0.0), jnp.where(lane == 121, row_col, 0.0))
    from_east = jnp.where(data, jnp.where(mine, 0.0, edges), jnp.where(lane == 122, row_col, 0.0))
    header = jnp.where(lane == 120, block_col + 1.0, 0.0)
    last = (
        dot(first, header.astype(BF16))
        + dot(one_hot(devices * 8, to_east), from_west.astype(BF16))
        + dot(one_hot(devices * 8, to_west), from_east.astype(BF16))
    )
    send(count // 2, last)
    for copy in sent:
        copy.wait()


def pack_records(forcing, tile, block, live, devices, n_lon):
    records, width = tile.shape[1], forcing.shape[1]
    levels = forcing.shape[0] // records // 2
    out = (devices, levels + 1, 8, width)
    return pl.pallas_call(
        functools.partial(pack_body, n_lon),
        name="pack_records",
        out_shape=pltpu.HBM(out, BF16),
        in_specs=[SMEM] + [HBM] * 3,
        out_specs=HBM,
        scratch_shapes=[
            pltpu.VMEM(tile.shape, jnp.int32),
            pltpu.VMEM(block.shape, jnp.int32),
            pltpu.VMEM(forcing.shape, BF16),
            pltpu.VMEM(out, BF16),
            pltpu.VMEM(forcing.shape, F32),
            pltpu.SemaphoreType.DMA((3,)),
            pltpu.SemaphoreType.DMA((levels + 1,)),
        ],
        compiler_params=pltpu.CompilerParams(vmem_limit_bytes=24 << 20),
    )(live, *map(hbm, (tile, block, forcing)))


STRIPS = 3


def strip_of(k):
    return k // 7, 18 * lax.rem(k, 7) if not isinstance(k, int) else 18 * (k % 7)


def turn(values, shift):
    if isinstance(shift, int):
        return pltpu.roll(values, shift % LANES, 1)
    return pltpu.roll(values, lax.rem(shift + 4 * LANES, LANES), 1)


def hbm(x):
    return pltpu.with_memory_space_constraint(x, pltpu.HBM)


def between(lane, low, high):
    return (lane >= low) & (lane < high)


def columns_body(
    adj_hbm, ef_hbm, nf_hbm, mask_hbm, out_ref, ocean_ref, adj_ref, flow_ref, mask, held, sems
):
    levels, rows = mask.shape[0], mask.shape[1]

    def moves(level):
        pairs = [(mask_hbm.at[level], mask.at[level])]
        pairs += [(adj_hbm.at[t, level], adj_ref.at[t, level]) for t in range(2)]
        pairs += [
            (
                source.at[level, :, pl.ds(x * LANES, LANES)],
                flow_ref.at[level, f, x],
            )
            for f, source in enumerate((ef_hbm, nf_hbm))
            for x in range(2)
        ]
        return [
            pltpu.make_async_copy(source, dest, sems.at[i, level])
            for i, (source, dest) in enumerate(pairs)
        ]

    for level in range(levels):
        for copy in moves(level):
            copy.start()
    lane = iota((rows, LANES), 1)
    held[...] = jnp.zeros_like(held)

    def put(tile, place, first, second):
        ends = jnp.where(lane < 64, first, second)
        inside = between(lane, 6 * place, 6 * place + 6)
        held[tile] = jnp.where(inside, turn(ends, 6 * place + 3), held[tile])

    def one(level, carry):
        for copy in moves(level):
            copy.wait()
        for x in range(2):
            ocean_ref[level, x] = mask[level, :, x * LANES : (x + 1) * LANES].astype(F32).astype(BF16)
        for t in range(2):
            put(0, t * levels + level, adj_ref[t, level, :, :LANES], adj_ref[t, level, :, LANES:])
        put(1, level, flow_ref[level, 0, 0], flow_ref[level, 0, 1])
        put(1, levels + level, flow_ref[level, 1, 0], flow_ref[level, 1, 1])
        put(2, level, mask[level, :, :LANES].astype(F32), mask[level, :, LANES:].astype(F32))
        return carry

    lax.fori_loop(0, levels, one, 0)
    for tile in range(3):
        out_ref[:, tile * LANES : (tile + 1) * LANES] = held[tile].astype(BF16)


def outer_columns(adj, ef, nf, mask):
    levels, rows, cells = ef.shape
    return pl.pallas_call(
        columns_body,
        name="outer_columns",
        out_shape=(
            jax.ShapeDtypeStruct((rows, 3 * LANES), BF16),
            jax.ShapeDtypeStruct((levels, 2, rows, LANES), BF16),
        ),
        in_specs=[HBM] * 4,
        out_specs=(VMEM,) * 2,
        scratch_shapes=[
            pltpu.VMEM(adj.shape, F32),
            pltpu.VMEM((levels, 2, 2, rows, LANES), F32),
            pltpu.VMEM(mask.shape, jnp.int32),
            pltpu.VMEM((3, rows, LANES), F32),
            pltpu.SemaphoreType.DMA((7, levels)),
        ],
        compiler_params=pltpu.CompilerParams(vmem_limit_bytes=24 << 20),
    )(*map(hbm, (adj, ef, nf, mask)))


def own_body(
    ef_hbm, nf_hbm, adj_hbm, ocean_ref,
    strips, spread_ref, rest_ref, first_ref, low_out, high_out,
    flow_ref, low, high, sems, adj_sem,
):
    levels, rows = ocean_ref.shape[0], ocean_ref.shape[2]

    def moves(level):
        return [
            pltpu.make_async_copy(
                source.at[level, :, pl.ds(x * LANES, LANES)],
                flow_ref.at[level, f, x],
                sems.at[2 * f + x, level],
            )
            for f, source in enumerate((ef_hbm, nf_hbm))
            for x in range(2)
        ]

    for level in range(levels):
        for copy in moves(level):
            copy.start()
    fetch = pltpu.make_async_copy(adj_hbm.at[0, pl.ds(0, KEPT)], first_ref, adj_sem)
    fetch.start()
    source, target = fiota((LANES, LANES), 0), fiota((1, LANES), 1)
    order = jnp.floor((target + 0.5) / 18.0)
    offset = target - 18.0 * order
    inner = jnp.where(offset < 3.0, offset, offset - 12.0)
    used = ((offset < 3.0) | (offset >= 15.0)) & (order < 7.0)
    for tile in range(STRIPS):
        k = order + 7.0 * tile
        level = jnp.where(k < levels, k, k - levels)
        live = used & (k < 2.0 * levels)
        for m, place in enumerate((k, level, level + levels)):
            hit = source == jnp.where(live, 6.0 * place + inner, -1.0)
            part = slice(tile * LANES, (tile + 1) * LANES)
            ones = jnp.where(hit, 1.0, 0.0).astype(BF16)
            if m == 0:
                spread_ref[:, part] = ones
            else:
                rest_ref[m - 1, :, part] = ones
    strips[...] = jnp.zeros_like(strips)
    low[...] = jnp.zeros_like(low)
    high[...] = jnp.zeros_like(high)
    lane = iota((rows, LANES), 1)

    def one(level, carry):
        for copy in moves(level):
            copy.wait()
        for f, ref in enumerate((flow_ref.at[level, 0], flow_ref.at[level, 1], ocean_ref.at[level])):
            ends = [ref[x].astype(F32) for x in range(2)]
            for x in range(2):
                here = slice(x * LANES, (x + 1) * LANES)
                low[level, 3 * f : 3 * f + 3, here] = ends[x][0:3]
                high[level, 3 * f : 3 * f + 3, here] = ends[x][rows - 3 : rows]
            own = jnp.where(lane < 9, turn(ends[0], 3), turn(ends[1], 15))
            for t in range(2):
                tile, first = strip_of(t * levels + level)
                keep = between(lane, first + 3, first + 15)
                strips[f, tile] = jnp.where(keep, turn(own, first), strips[f, tile])
        return carry

    for level in range(levels):
        one(level, 0)
    low_out[...] = low[...].astype(BF16)
    high_out[...] = high[...].astype(BF16)
    fetch.wait()


def own_strips(ef, nf, adj, ocean):
    levels, rows = ef.shape[0], ef.shape[1]
    return pl.pallas_call(
        own_body,
        name="own_strips",
        out_shape=(
            jax.ShapeDtypeStruct((3, STRIPS, rows, LANES), F32),
            jax.ShapeDtypeStruct((LANES, STRIPS * LANES), BF16),
            jax.ShapeDtypeStruct((2, LANES, STRIPS * LANES), BF16),
            jax.ShapeDtypeStruct((KEPT,) + adj.shape[2:], F32),
            jax.ShapeDtypeStruct((levels, 16, 2 * LANES), BF16),
            jax.ShapeDtypeStruct((levels, 16, 2 * LANES), BF16),
        ),
        in_specs=[HBM, HBM, HBM, VMEM],
        out_specs=(VMEM,) * 6,
        scratch_shapes=[
            pltpu.VMEM((levels, 2, 2, rows, LANES), F32),
            pltpu.VMEM((levels, 16, 2 * LANES), F32),
            pltpu.VMEM((levels, 16, 2 * LANES), F32),
            pltpu.SemaphoreType.DMA((4, levels)),
            pltpu.SemaphoreType.DMA,
        ],
        cost_estimate=pl.CostEstimate(flops=10**8, bytes_accessed=10**7, transcendentals=0),
        compiler_params=pltpu.CompilerParams(vmem_limit_bytes=24 << 20),
    )(hbm(ef), hbm(nf), hbm(adj), ocean)


def edges_body(
    west, east, own_ref, spread_ref, rest_ref, low_main, high_main,
    strips, adj, low_out, high_out, held,
):
    levels, rows = low_main.shape[0], own_ref.shape[2]

    def halo(tile, m):
        part = slice(tile * LANES, (tile + 1) * LANES)
        theirs, ours = west[:, part].astype(F32), east[:, part].astype(F32)
        merged = jnp.where(west_lane(theirs.shape), theirs, ours).astype(BF16)
        return dot(merged, rest_ref[m - 1] if m else spread_ref[...])

    for f, (source, m) in enumerate(((1, 1), (1, 2), (2, 1))):
        halos = halo(source, m)
        for tile in range(STRIPS):
            strips[f, tile] = own_ref[f, tile] + halos[:, tile * LANES : (tile + 1) * LANES]
    halos = halo(0, 0)
    for tile in range(STRIPS):
        adj[tile] = halos[:, tile * LANES : (tile + 1) * LANES].astype(BF16)
    held[...] = jnp.zeros_like(held)
    for side, (out, main, first) in enumerate(
        ((low_out, low_main, 0), (high_out, high_main, rows - 3))
    ):
        at = slice(first, first + 3)
        for f in range(3):
            here = slice(3 * f, 3 * f + 3)
            held[side, 0, here, :LANES] = strips[f, 0, at, :]
            held[side, 0, here, LANES:] = strips[f, 1, at, :]
            held[side, 1, here, :LANES] = strips[f, 2, at, :]
        out[0:levels] = main[...]
        out[levels : levels + 2] = held[side].astype(BF16)


def outer_rows(west, east, own, spread, rest, low, high):
    edge = (low.shape[0] + 2,) + low.shape[1:]
    return pl.pallas_call(
        edges_body,
        name="outer_rows",
        out_shape=(
            jax.ShapeDtypeStruct(own.shape, F32),
            jax.ShapeDtypeStruct(own.shape[1:], BF16),
            jax.ShapeDtypeStruct(edge, BF16),
            jax.ShapeDtypeStruct(edge, BF16),
        ),
        in_specs=[VMEM] * 7,
        out_specs=(VMEM,) * 4,
        scratch_shapes=[pltpu.VMEM((2, 2) + low.shape[1:], F32)],
        compiler_params=pltpu.CompilerParams(vmem_limit_bytes=24 << 20),
    )(west, east, own, spread, rest, low, high)


def place_body(
    odd_ref,
    arrived_ref,
    first_ref,
    adj_hbm,
    ocean_ref,
    strip_ref,
    fields_ref,
    spread_ref,
    state_ref,
    out_strip_ref,
    swap_a_ref,
    swap_b_ref,
    second_ref,
    hot,
    low,
    high,
    sems,
):
    devices = arrived_ref.shape[0]
    slots = devices * 8
    levels, rows = ocean_ref.shape[0], first_ref.shape[1]
    part = levels // 2
    late = levels - KEPT
    fetch = [
        pltpu.make_async_copy(
            adj_hbm.at[1, pl.ds(i * part, part)], second_ref.at[pl.ds(i * part, part)], sems.at[i]
        )
        for i in range(2)
    ]
    rest = pltpu.make_async_copy(
        adj_hbm.at[0, pl.ds(KEPT, late)], second_ref.at[pl.ds(levels, late)], sems.at[2]
    )
    for copy in [rest] + fetch:
        copy.start()
    last = arrived_ref[:, levels].astype(F32).reshape(slots, LANES)
    heads = last.T[120:128]
    later = pltpu.roll(heads, 4, 1)
    row = fiota((rows, slots), 0)
    for b, source in enumerate((heads, later)):
        for c in range(2):
            found = source[0:1] == 2.0 * row + (c + 1.0)
            hot[pl.ds((2 * b + c) * rows, rows), :] = jnp.where(found, 1.0, 0.0).astype(BF16)
    lane = iota((slots, LANES), 1)
    mine = west_lane((slots, LANES))
    from_west = jnp.where(mine & (lane < 120), last, 0.0).astype(BF16)
    from_east = jnp.where(mine | (lane >= 120), 0.0, last).astype(BF16)
    spread = spread_ref[...]
    strips = dot(one_hot(rows, heads[1:2] - 1.0), dot(from_west, spread).astype(BF16)) + dot(
        one_hot(rows, heads[2:3] - 1.0), dot(from_east, spread).astype(BF16)
    )
    for tile in range(STRIPS):
        out_strip_ref[tile] = strip_ref[tile].astype(F32) + strips[:, tile * LANES : (tile + 1) * LANES]
    low[...] = jnp.zeros_like(low)
    high[...] = jnp.zeros_like(high)
    wide = iota((rows, LANES), 1)

    def one(t, level):
        values = arrived_ref[:, level].astype(F32).reshape(slots, LANES).astype(BF16)
        k = t * levels + level
        tile, first = strip_of(k)
        ends = []
        for c in range(2):
            part = slice(c * LANES, (c + 1) * LANES)
            forced = dot(hot[pl.ds((2 * t + c) * rows, rows), :], values)
            before = first_ref[level, :, part] if t == 0 and level < KEPT else second_ref[level if t == 1 else levels + level - KEPT, :, part]
            total = before + forced
            ends.append(total)
            masked = total * ocean_ref[level, c].astype(F32)
            state_ref[k, c] = masked
            low[level, 3 * t : 3 * t + 3, part] = masked[0:3]
            high[level, 3 * t : 3 * t + 3, part] = masked[rows - 3 : rows]
        held = out_strip_ref[tile]
        held = jnp.where(between(wide, first + 3, first + 9), turn(ends[0], first + 3), held)
        out_strip_ref[tile] = jnp.where(
            between(wide, first + 9, first + 15), turn(ends[1], first + 15), held
        )

    for t in range(2):
        for level in range(levels):
            if t == 0 and level == KEPT:
                rest.wait()
            if t == 1 and level % part == 0:
                fetch[level // part].wait()
            one(t, level)
    for tile in range(STRIPS):
        out_strip_ref[tile] = out_strip_ref[tile] * fields_ref[2, tile]
    for out, side in ((low, slice(0, 3)), (high, slice(rows - 3, rows))):
        out[levels, 0:3, :LANES] = out_strip_ref[0, side, :]
        out[levels, 0:3, LANES:] = out_strip_ref[1, side, :]
        out[levels, 3:6, :LANES] = out_strip_ref[2, side, :]
    odd = odd_ref[0] == 1
    swap_a_ref[...] = jnp.where(odd, low[...], high[...]).astype(BF16)
    swap_b_ref[...] = jnp.where(odd, high[...], low[...]).astype(BF16)


def place_records(odd, arrived, first, adj, ocean, strip, fields, spread):
    levels, rows, cells = adj.shape[1:]
    devices = arrived.shape[0]
    edge = jax.ShapeDtypeStruct((levels + 1, 8, cells), BF16)
    return pl.pallas_call(
        place_body,
        name="place_records",
        out_shape=(
            jax.ShapeDtypeStruct((2 * levels, 2, rows, LANES), F32),
            jax.ShapeDtypeStruct((STRIPS, rows, LANES), F32),
            edge,
            edge,
        ),
        in_specs=[SMEM, VMEM, VMEM, HBM] + [VMEM] * 4,
        out_specs=(VMEM,) * 4,
        scratch_shapes=[
            pltpu.VMEM((2 * levels - KEPT, rows, cells), F32),
            pltpu.VMEM((4 * rows, devices * 8), BF16),
            pltpu.VMEM(edge.shape, F32),
            pltpu.VMEM(edge.shape, F32),
            pltpu.SemaphoreType.DMA((3,)),
        ],
        compiler_params=pltpu.CompilerParams(vmem_limit_bytes=24 << 20),
    )(odd, arrived, first, hbm(adj), ocean, strip, fields, spread)


def steps_body(
    where_ref,
    spread_ref,
    state_ref,
    strip_ref,
    swap_a_ref,
    swap_b_ref,
    ef_hbm,
    nf_hbm,
    ocean_ref,
    fields_ref,
    low_ref,
    high_ref,
    out_ref,
    flow_all,
    ocean,
    strip_flow,
    strip_ocean,
    coef,
    cells_a,
    cells_b,
    cells_c,
    patch,
    below,
    above,
    rows_low,
    rows_high,
    done,
    sems,
    level_sems,
):
    levels, rows = ocean_ref.shape[0], ocean_ref.shape[2]

    groups = ((0, 2), (2, levels))

    def arrivals(group):
        first, end = groups[group]
        span = pl.ds(first, end - first)
        return [
            pltpu.make_async_copy(
                source.at[span, :, pl.ds(x * LANES, LANES)],
                flow_all.at[span, f, x, pl.ds(16, rows), :],
                level_sems.at[2 * f + x, group],
            )
            for f, source in enumerate((ef_hbm, nf_hbm))
            for x in range(2)
        ]

    for group in range(2):
        for copy in arrivals(group):
            copy.start()
    tall = rows + 16
    inner = slice(16, 16 + rows)
    before, after = slice(13, 16), slice(16 + rows, 19 + rows)
    at_start, at_end, odd = where_ref[0], where_ref[1], where_ref[2] == 1
    lane, sub = iota((8, LANES), 1), iota((8, LANES), 0)
    for ref in (strip_flow.at[0], strip_flow.at[1], strip_ocean):
        ref[0, 0:16] = jnp.zeros((16, LANES), F32)
        ref[0, 16 + rows : 32 + rows] = jnp.zeros((16, LANES), F32)
    for x in range(2):
        ocean[x, 0:16] = jnp.zeros((16, LANES), F32)
        ocean[x, 16 + rows : 32 + rows] = jnp.zeros((16, LANES), F32)
    for ref in (cells_a, cells_b, cells_c):
        for t in range(2):
            for x in range(2):
                ref[t, x, 0:16] = jnp.zeros((16, LANES), F32)
                ref[t, x, 16 + rows : 32 + rows] = jnp.zeros((16, LANES), F32)
    below[...] = jnp.where(odd, swap_a_ref[...].astype(F32), swap_b_ref[...].astype(F32))
    above[...] = jnp.where(odd, swap_b_ref[...].astype(F32), swap_a_ref[...].astype(F32))
    rows_low[...] = low_ref[...].astype(F32)
    rows_high[...] = high_ref[...].astype(F32)
    top = 8 + rows
    shut_s = (sub == 0) & (at_start == 1)
    shut_n = (sub == 7) & (at_end == 1)

    def close_top(ref):
        ref[top : top + 8] = jnp.where(shut_n, 0.0, ref[top : top + 8])

    def prepare(x, i, flow, here, turned):
        at = slice(8 * i, 8 * i + 8)
        ce = jnp.maximum(here, 0.0)
        cw = -jnp.minimum(turned, 0.0)
        cn = jnp.maximum(flow[1, x, at], 0.0)
        cs = -jnp.minimum(flow[1, x, 8 * i - 1 : 8 * i + 7], 0.0)
        coef[0, x, at] = ce
        coef[1, x, at] = cw
        coef[2, x, at] = cn
        coef[3, x, at] = cs
        coef[4, x, at] = 1.0 - ce - cw - cn - cs

    def around_k(i, k):
        total = 4.0 * k
        if i == 2:
            total = total - jnp.where(shut_s, k, 0.0)
        if i == 1 + rows // 8:
            total = total - jnp.where(shut_n, k, 0.0)
        return total

    def update(source, x, i, k, here, east, west):
        at = slice(8 * i, 8 * i + 8)
        north = source[x, 8 * i + 1 : 8 * i + 9]
        south = source[x, 8 * i - 1 : 8 * i + 7]
        return (
            (coef[4, x, at] - around_k(i, k)) * here
            + (coef[0, x, at] + k) * east
            + (coef[1, x, at] + k) * west
            + (coef[2, x, at] + k) * north
            + (coef[3, x, at] + k) * south
        )

    def tiles(step):
        edge = 1 if step == STEPS - 1 else 0
        return range(1 + edge, 1 + tall // 8 - edge)

    for tile in range(STRIPS):
        k = jnp.zeros((1, LANES), F32)
        for s in range(7):
            slice_id = 7 * tile + s
            if slice_id < 2 * levels:
                own = between(iota((1, LANES), 1), 18 * s, 18 * s + 18)
                k = jnp.where(own, spread_ref[slice_id // levels, slice_id % levels], k)
        block = levels + tile // 2
        part = slice((tile % 2) * LANES, (tile % 2 + 1) * LANES)
        for f, dest in enumerate((strip_flow.at[0, 0], strip_flow.at[1, 0], strip_ocean.at[0])):
            dest[before] = rows_low[block, 3 * f : 3 * f + 3, part]
            dest[inner] = fields_ref[f, tile]
            dest[after] = rows_high[block, 3 * f : 3 * f + 3, part]
        close_top(strip_flow.at[1, 0])
        for i in range(1, 1 + tall // 8):
            face = strip_flow[0, 0, 8 * i : 8 * i + 8]
            prepare(0, i, strip_flow, face, pltpu.roll(face, 1, 1))
        here = slice(3 * (tile // 2), 3 * (tile // 2) + 3)
        cells_a[0, 0, before] = below[levels, here, part]
        cells_a[0, 0, inner] = strip_ref[tile]
        cells_a[0, 0, after] = above[levels, here, part]
        source = cells_a.at[0]
        for step in range(STEPS):
            dest = (cells_b, cells_c, None)[step]
            for i in tiles(step):
                at = slice(8 * i, 8 * i + 8)
                value = source[0, at]
                total = update(
                    source, 0, i, k, value, pltpu.roll(value, LANES - 1, 1), pltpu.roll(value, 1, 1)
                )
                if dest is None:
                    patch[tile, 8 * i - 16 : 8 * i - 8] = total
                else:
                    dest[0, 0, at] = total * strip_ocean[0, at]
            source = dest.at[0] if dest is not None else None

    def leave(level):
        return pltpu.make_async_copy(done.at[:, level], out_ref.at[:, level], sems.at[level])

    def one(level, carry):
        flow = flow_all.at[level]
        for group in range(2):

            @pl.when(level == groups[group][0])
            def _():
                for copy in arrivals(group):
                    copy.wait()

        for f in range(2):
            for x in range(2):
                flow[f, x, 0:16] = jnp.zeros((16, LANES), F32)
                flow[f, x, 16 + rows : 32 + rows] = jnp.zeros((16, LANES), F32)
        for x in range(2):
            part = slice(x * LANES, (x + 1) * LANES)
            ocean[x, inner] = ocean_ref[level, x].astype(F32)
            for f, dest in enumerate((flow.at[0, x], flow.at[1, x], ocean.at[x])):
                dest[before] = rows_low[level, 3 * f : 3 * f + 3, part]
                dest[after] = rows_high[level, 3 * f : 3 * f + 3, part]
            close_top(flow.at[1, x])
            for t in range(2):
                cells_a[t, x, before] = below[level, 3 * t : 3 * t + 3, part]
                cells_a[t, x, inner] = state_ref[t * levels + level, x]
                cells_a[t, x, after] = above[level, 3 * t : 3 * t + 3, part]
        for i in range(1, 1 + tall // 8):
            at = slice(8 * i, 8 * i + 8)
            faces = [flow[0, x, at] for x in range(2)]
            turned = [pltpu.roll(v, 1, 1) for v in faces]
            turned[1] = jnp.where(lane == 0, turned[0], turned[1])
            for x in range(2):
                prepare(x, i, flow, faces[x], turned[x])
        ks = [spread_ref[t, level] for t in range(2)]
        spots = [strip_of(t * levels + level) for t in range(2)]
        buffers = (cells_a, cells_b, cells_c)
        for step in range(STEPS):
            for i in tiles(step):
                at = slice(8 * i, 8 * i + 8)
                for t in range(2):
                    source = buffers[step].at[t]
                    here = [source[x, at] for x in range(2)]
                    right = [pltpu.roll(v, LANES - 1, 1) for v in here]
                    left = [pltpu.roll(v, 1, 1) for v in here]
                    east = [jnp.where(lane == LANES - 1, right[1], right[0]), right[1]]
                    west = [left[0], jnp.where(lane == 0, left[0], left[1])]
                    for x in range(2):
                        total = update(source, x, i, ks[t], here[x], east[x], west[x])
                        if step < STEPS - 1:
                            buffers[step + 1][t, x, at] = total * ocean[x, at]
                            continue
                        tile, first = spots[t]
                        shift, keep = (125 - first, lane < 3) if x == 0 else (113 - first, lane >= 125)
                        fixed = turn(patch[tile, 8 * i - 16 : 8 * i - 8], shift)
                        done[t, level, 8 * i - 16 : 8 * i - 8, x * LANES : (x + 1) * LANES] = (
                            jnp.where(keep, fixed, total)
                        )
        leave(level).start()
        return carry

    lax.fori_loop(0, levels, one, 0)
    for level in range(levels):
        leave(level).wait()


def run_steps(where, spread, state, strip, swap_a, swap_b, ef, nf, ocean, fields, low, high):
    levels, rows = ocean.shape[0], ocean.shape[2]
    tall, width = rows + 32, 2 * LANES
    buffer = pltpu.VMEM((2, 2, tall, LANES), F32)
    return pl.pallas_call(
        steps_body,
        name="three_steps",
        out_shape=jax.ShapeDtypeStruct((2, levels, rows, width), F32),
        in_specs=[SMEM, SMEM] + [VMEM] * 4 + [HBM] * 2 + [VMEM] * 4,
        out_specs=HBM,
        scratch_shapes=[
            pltpu.VMEM((levels, 2, 2, tall, LANES), F32),
            pltpu.VMEM((2, tall, LANES), F32),
            pltpu.VMEM((2, 1, tall, LANES), F32),
            pltpu.VMEM((1, tall, LANES), F32),
            pltpu.VMEM((5, 2, tall, LANES), F32),
            buffer,
            buffer,
            buffer,
            pltpu.VMEM((STRIPS, rows, LANES), F32),
            pltpu.VMEM(swap_a.shape, F32),
            pltpu.VMEM(swap_a.shape, F32),
            pltpu.VMEM(low.shape, F32),
            pltpu.VMEM(low.shape, F32),
            pltpu.VMEM((2, levels, rows, width), F32),
            pltpu.SemaphoreType.DMA((levels,)),
            pltpu.SemaphoreType.DMA((4, 2)),
        ],
        compiler_params=pltpu.CompilerParams(vmem_limit_bytes=24 << 20),
    )(where, spread, state, strip, swap_a, swap_b, hbm(ef), hbm(nf), ocean, fields, low, high)


def around(block, axis, distance):
    count = lax.axis_size(axis)
    return lax.ppermute(block, axis, [(i, (i + distance) % count) for i in range(count)])


def along(block, axis, distance):
    count = lax.axis_size(axis)
    route = [(i, i + distance) for i in range(count) if 0 <= i + distance < count]
    return lax.ppermute(block, axis, route)


def swapped(block, axis, start):
    count = lax.axis_size(axis)
    lower = range(start, count - 1, 2)
    return lax.ppermute(block, axis, [(i, i + 1) for i in lower] + [(i + 1, i) for i in lower])


def per_device(
    adjoint_in,
    east_flow,
    north_flow,
    diffusivity,
    land_mask,
    forcing,
    obs_tile,
    obs_block,
    obs_live,
):
    n_lat, n_lon = lax.axis_size("lat"), lax.axis_size("lon")
    lat = lax.axis_index("lat")
    odd = lat % 2
    where = jnp.stack([lat == 0, lat == n_lat - 1, odd == 1]).astype(jnp.int32)
    flat = forcing.transpose(0, 1, 3, 2, 4).reshape(-1, forcing.shape[4])
    packed = pack_records(flat, obs_tile, obs_block, obs_live, n_lat * n_lon, n_lon)
    arrived = lax.all_to_all(packed, ("lat", "lon"), split_axis=0, concat_axis=0, tiled=True)
    columns, ocean = outer_columns(adjoint_in, east_flow, north_flow, land_mask)
    west = around(columns, "lon", 1)
    east = around(columns, "lon", -1)
    own, spread, rest, adj_first, low, high = own_strips(
        east_flow, north_flow, adjoint_in, ocean
    )
    fields, adj_strip, low, high = outer_rows(west, east, own, spread, rest, low, high)
    below = along(high, "lat", 1)
    above = along(low, "lat", -1)
    state, strip, swap_a, swap_b = place_records(
        odd.reshape(1).astype(jnp.int32), arrived, adj_first, adjoint_in, ocean, adj_strip, fields, spread
    )
    swap_a = swapped(swap_a, "lat", 0)
    swap_b = swapped(swap_b, "lat", 1)
    return run_steps(
        where,
        diffusivity,
        state,
        strip,
        swap_a,
        swap_b,
        east_flow,
        north_flow,
        ocean,
        fields,
        below,
        above,
    )


def solution(mesh):
    in_specs = (
        P(None, None, "lat", "lon"),
        P(None, "lat", "lon"),
        P(None, "lat", "lon"),
        P(),
        P(None, "lat", "lon"),
        P(("lat", "lon"), None, None, None, None),
        P(("lat", "lon"), None),
        P(("lat", "lon"), None),
        P(("lat", "lon")),
    )
    out_specs = P(None, None, "lat", "lon")
    return jax.shard_map(
        per_device, mesh=mesh, in_specs=in_specs, out_specs=out_specs, check_vma=False
    )
```

```python
import functools

import jax
import jax.numpy as jnp
from jax import lax
from jax.experimental import pallas as pl
from jax.experimental.pallas import tpu as pltpu
from jax.sharding import PartitionSpec as P

STEPS = 3
LANES = 128
KEPT = 9
F32 = jnp.float32
BF16 = jnp.bfloat16
HBM = pl.BlockSpec(memory_space=pltpu.HBM)
VMEM = pl.BlockSpec(memory_space=pltpu.VMEM)
SMEM = pl.BlockSpec(memory_space=pltpu.SMEM)


def iota(shape, dim):
    return lax.broadcasted_iota(jnp.int32, shape, dim)


def fiota(shape, dim):
    return iota(shape, dim).astype(F32)


def west_lane(shape):
    lane = fiota(shape, 1)
    return lane - 6.0 * jnp.floor((lane + 0.5) / 6.0) < 3.0


def one_hot(rows, code):
    shape = (rows, code.shape[1])
    return jnp.where(fiota(shape, 0) == code, 1.0, 0.0).astype(BF16)


def dot(a, b):
    return jnp.dot(a, b, preferred_element_type=F32)


def pack_body(
    n_lon, live_ref, tile_in, block_in, forcing_in, out_hbm,
    tile_ref, block_ref, forcing_ref, out_ref, wide, sems, out_sems,
):
    records, devices = tile_ref.shape[1], out_ref.shape[0]
    count = forcing_ref.shape[0] // records
    levels = count // 2
    moves = [
        pltpu.make_async_copy(source, dest, sems.at[i])
        for i, (source, dest) in enumerate(
            (
                (tile_in, tile_ref),
                (block_in, block_ref),
                (forcing_in, forcing_ref),
            )
        )
    ]
    for move in moves:
        move.start()
    for move in moves[:2]:
        move.wait()
    tile = tile_ref[...].astype(F32)
    block = block_ref[...].astype(F32)
    square = (records, records)
    low, high = iota(square, 0), iota(square, 1)
    tile_col = jnp.sum(jnp.where(low == high, tile, 0.0), axis=1, keepdims=True)
    block_col = jnp.sum(jnp.where(low == high, block, 0.0), axis=1, keepdims=True)
    earlier = jnp.where((tile_col == tile) & (low < high), 1.0, 0.0)
    rank = jnp.sum(earlier, axis=0, keepdims=True)
    live = iota((1, records), 1) < live_ref[0]
    band = jnp.floor((tile + 0.5) / n_lon) * n_lon
    column = tile - band
    east = band + jnp.where(column == n_lon - 1, 0.0, column + 1.0)
    west = band + jnp.where(column == 0.0, n_lon - 1.0, column - 1.0)
    half = block - 2.0 * jnp.floor(block * 0.5)
    code = jnp.where(live, tile * 4.0 + rank, -8.0)
    to_east = jnp.where(live & (half == 1.0), east * 4.0 + rank, -8.0)
    to_west = jnp.where(live & (half == 0.0), west * 4.0 + rank, -8.0)
    moves[2].wait()
    wide[...] = forcing_ref[...].astype(F32)
    sent = []

    def send(q, values):
        out_ref[:, q] = values.astype(BF16).reshape(devices, 4, LANES)
        if q % 2 == 1 or q == count:
            span = pl.ds(q, 1) if q == count else pl.ds(q - 1, 2)
            copy = pltpu.make_async_copy(
                out_ref.at[:, span], out_hbm.at[:, span], out_sems.at[q // 2]
            )
            copy.start()
            sent.append(copy)

    first = one_hot(devices * 4, code)
    lane = iota((records, LANES), 1)
    edges = jnp.zeros((records, LANES), F32)
    for place in range(count):
        level, t = divmod(place, 2)
        k = t * levels + level
        values = wide[pl.ds(place, records, stride=count), :]
        turned = pltpu.roll(values, (6 * k + 3) % LANES, 1)
        edges = jnp.where((lane >= 6 * k) & (lane < 6 * k + 6), turned, edges)
        send(place, dot(first, values.astype(BF16)))
    row_col = jnp.floor(block_col * 0.5) + 1.0
    mine = west_lane((records, LANES))
    data = lane < 6 * count
    from_west = jnp.where(data, jnp.where(mine, edges, 0.0), jnp.where(lane == 121, row_col, 0.0))
    from_east = jnp.where(data, jnp.where(mine, 0.0, edges), jnp.where(lane == 122, row_col, 0.0))
    header = jnp.where(lane == 120, block_col + 1.0, 0.0)
    last = (
        dot(first, header.astype(BF16))
        + dot(one_hot(devices * 4, to_east), from_west.astype(BF16))
        + dot(one_hot(devices * 4, to_west), from_east.astype(BF16))
    )
    send(count, last)
    for copy in sent:
        copy.wait()


def pack_records(forcing, tile, block, live, devices, n_lon):
    records, width = tile.shape[1], forcing.shape[1]
    levels = forcing.shape[0] // records // 2
    out = (devices, 2 * levels + 1, 4, width)
    return pl.pallas_call(
        functools.partial(pack_body, n_lon),
        name="pack_records",
        out_shape=pltpu.HBM(out, BF16),
        in_specs=[SMEM] + [HBM] * 3,
        out_specs=HBM,
        scratch_shapes=[
            pltpu.VMEM(tile.shape, jnp.int32),
            pltpu.VMEM(block.shape, jnp.int32),
            pltpu.VMEM(forcing.shape, BF16),
            pltpu.VMEM(out, BF16),
            pltpu.VMEM(forcing.shape, F32),
            pltpu.SemaphoreType.DMA((3,)),
            pltpu.SemaphoreType.DMA((levels + 1,)),
        ],
        compiler_params=pltpu.CompilerParams(vmem_limit_bytes=24 << 20),
    )(live, *map(hbm, (tile, block, forcing)))


STRIPS = 3


def strip_of(k):
    return k // 7, 18 * lax.rem(k, 7) if not isinstance(k, int) else 18 * (k % 7)


def turn(values, shift):
    if isinstance(shift, int):
        return pltpu.roll(values, shift % LANES, 1)
    return pltpu.roll(values, lax.rem(shift + 4 * LANES, LANES), 1)


def hbm(x):
    return pltpu.with_memory_space_constraint(x, pltpu.HBM)


def between(lane, low, high):
    return (lane >= low) & (lane < high)


def columns_body(
    adj_hbm, ef_hbm, nf_hbm, mask_hbm, out_ref, ocean_ref, adj_ref, flow_ref, mask, held, sems
):
    levels, rows = mask.shape[0], mask.shape[1]

    def moves(level):
        pairs = [(mask_hbm.at[level], mask.at[level])]
        pairs += [(adj_hbm.at[t, level], adj_ref.at[t, level]) for t in range(2)]
        pairs += [
            (
                source.at[level, :, pl.ds(x * LANES, LANES)],
                flow_ref.at[level, f, x],
            )
            for f, source in enumerate((ef_hbm, nf_hbm))
            for x in range(2)
        ]
        return [
            pltpu.make_async_copy(source, dest, sems.at[i, level])
            for i, (source, dest) in enumerate(pairs)
        ]

    for level in range(levels):
        for copy in moves(level):
            copy.start()
    lane = iota((rows, LANES), 1)
    held[...] = jnp.zeros_like(held)

    def put(tile, place, first, second):
        ends = jnp.where(lane < 64, first, second)
        inside = between(lane, 6 * place, 6 * place + 6)
        held[tile] = jnp.where(inside, turn(ends, 6 * place + 3), held[tile])

    def one(level, carry):
        for copy in moves(level):
            copy.wait()
        for x in range(2):
            ocean_ref[level, x] = mask[level, :, x * LANES : (x + 1) * LANES].astype(F32).astype(BF16)
        for t in range(2):
            put(0, t * levels + level, adj_ref[t, level, :, :LANES], adj_ref[t, level, :, LANES:])
        put(1, level, flow_ref[level, 0, 0], flow_ref[level, 0, 1])
        put(1, levels + level, flow_ref[level, 1, 0], flow_ref[level, 1, 1])
        put(2, level, mask[level, :, :LANES].astype(F32), mask[level, :, LANES:].astype(F32))
        return carry

    lax.fori_loop(0, levels, one, 0)
    for tile in range(3):
        out_ref[:, tile * LANES : (tile + 1) * LANES] = held[tile].astype(BF16)


def outer_columns(adj, ef, nf, mask):
    levels, rows, cells = ef.shape
    return pl.pallas_call(
        columns_body,
        name="outer_columns",
        out_shape=(
            jax.ShapeDtypeStruct((rows, 3 * LANES), BF16),
            jax.ShapeDtypeStruct((levels, 2, rows, LANES), BF16),
        ),
        in_specs=[HBM] * 4,
        out_specs=(VMEM,) * 2,
        scratch_shapes=[
            pltpu.VMEM(adj.shape, F32),
            pltpu.VMEM((levels, 2, 2, rows, LANES), F32),
            pltpu.VMEM(mask.shape, jnp.int32),
            pltpu.VMEM((3, rows, LANES), F32),
            pltpu.SemaphoreType.DMA((7, levels)),
        ],
        compiler_params=pltpu.CompilerParams(vmem_limit_bytes=24 << 20),
    )(*map(hbm, (adj, ef, nf, mask)))


def own_body(
    ef_hbm, nf_hbm, adj_hbm, ocean_ref,
    strips, spread_ref, rest_ref, first_ref, low_out, high_out,
    flow_ref, low, high, sems, adj_sem,
):
    levels, rows = ocean_ref.shape[0], ocean_ref.shape[2]

    def moves(level):
        return [
            pltpu.make_async_copy(
                source.at[level, :, pl.ds(x * LANES, LANES)],
                flow_ref.at[level, f, x],
                sems.at[2 * f + x, level],
            )
            for f, source in enumerate((ef_hbm, nf_hbm))
            for x in range(2)
        ]

    for level in range(levels):
        for copy in moves(level):
            copy.start()
    fetch = pltpu.make_async_copy(adj_hbm.at[0, pl.ds(0, KEPT)], first_ref, adj_sem)
    fetch.start()
    source, target = fiota((LANES, LANES), 0), fiota((1, LANES), 1)
    order = jnp.floor((target + 0.5) / 18.0)
    offset = target - 18.0 * order
    inner = jnp.where(offset < 3.0, offset, offset - 12.0)
    used = ((offset < 3.0) | (offset >= 15.0)) & (order < 7.0)
    for tile in range(STRIPS):
        k = order + 7.0 * tile
        level = jnp.where(k < levels, k, k - levels)
        live = used & (k < 2.0 * levels)
        for m, place in enumerate((k, level, level + levels)):
            hit = source == jnp.where(live, 6.0 * place + inner, -1.0)
            part = slice(tile * LANES, (tile + 1) * LANES)
            ones = jnp.where(hit, 1.0, 0.0).astype(BF16)
            if m == 0:
                spread_ref[:, part] = ones
            else:
                rest_ref[m - 1, :, part] = ones
    strips[...] = jnp.zeros_like(strips)
    low[...] = jnp.zeros_like(low)
    high[...] = jnp.zeros_like(high)
    lane = iota((rows, LANES), 1)

    def one(level, carry):
        for copy in moves(level):
            copy.wait()
        for f, ref in enumerate((flow_ref.at[level, 0], flow_ref.at[level, 1], ocean_ref.at[level])):
            ends = [ref[x].astype(F32) for x in range(2)]
            for x in range(2):
                here = slice(x * LANES, (x + 1) * LANES)
                low[level, 3 * f : 3 * f + 3, here] = ends[x][0:3]
                high[level, 3 * f : 3 * f + 3, here] = ends[x][rows - 3 : rows]
            own = jnp.where(lane < 9, turn(ends[0], 3), turn(ends[1], 15))
            for t in range(2):
                tile, first = strip_of(t * levels + level)
                keep = between(lane, first + 3, first + 15)
                strips[f, tile] = jnp.where(keep, turn(own, first), strips[f, tile])
        return carry

    for level in range(levels):
        one(level, 0)
    low_out[...] = low[...].astype(BF16)
    high_out[...] = high[...].astype(BF16)
    fetch.wait()


def own_strips(ef, nf, adj, ocean):
    levels, rows = ef.shape[0], ef.shape[1]
    return pl.pallas_call(
        own_body,
        name="own_strips",
        out_shape=(
            jax.ShapeDtypeStruct((3, STRIPS, rows, LANES), F32),
            jax.ShapeDtypeStruct((LANES, STRIPS * LANES), BF16),
            jax.ShapeDtypeStruct((2, LANES, STRIPS * LANES), BF16),
            jax.ShapeDtypeStruct((KEPT,) + adj.shape[2:], F32),
            jax.ShapeDtypeStruct((levels, 16, 2 * LANES), BF16),
            jax.ShapeDtypeStruct((levels, 16, 2 * LANES), BF16),
        ),
        in_specs=[HBM, HBM, HBM, VMEM],
        out_specs=(VMEM,) * 6,
        scratch_shapes=[
            pltpu.VMEM((levels, 2, 2, rows, LANES), F32),
            pltpu.VMEM((levels, 16, 2 * LANES), F32),
            pltpu.VMEM((levels, 16, 2 * LANES), F32),
            pltpu.SemaphoreType.DMA((4, levels)),
            pltpu.SemaphoreType.DMA,
        ],
        cost_estimate=pl.CostEstimate(flops=10**8, bytes_accessed=10**7, transcendentals=0),
        compiler_params=pltpu.CompilerParams(vmem_limit_bytes=24 << 20),
    )(hbm(ef), hbm(nf), hbm(adj), ocean)


def edges_body(
    west, east, own_ref, spread_ref, rest_ref, low_main, high_main,
    strips, adj, low_out, high_out, held,
):
    levels, rows = low_main.shape[0], own_ref.shape[2]

    def halo(tile, m):
        part = slice(tile * LANES, (tile + 1) * LANES)
        theirs, ours = west[:, part].astype(F32), east[:, part].astype(F32)
        merged = jnp.where(west_lane(theirs.shape), theirs, ours).astype(BF16)
        return dot(merged, rest_ref[m - 1] if m else spread_ref[...])

    for f, (source, m) in enumerate(((1, 1), (1, 2), (2, 1))):
        halos = halo(source, m)
        for tile in range(STRIPS):
            strips[f, tile] = own_ref[f, tile] + halos[:, tile * LANES : (tile + 1) * LANES]
    halos = halo(0, 0)
    for tile in range(STRIPS):
        adj[tile] = halos[:, tile * LANES : (tile + 1) * LANES].astype(BF16)
    held[...] = jnp.zeros_like(held)
    for side, (out, main, first) in enumerate(
        ((low_out, low_main, 0), (high_out, high_main, rows - 3))
    ):
        at = slice(first, first + 3)
        for f in range(3):
            here = slice(3 * f, 3 * f + 3)
            held[side, 0, here, :LANES] = strips[f, 0, at, :]
            held[side, 0, here, LANES:] = strips[f, 1, at, :]
            held[side, 1, here, :LANES] = strips[f, 2, at, :]
        out[0:levels] = main[...]
        out[levels : levels + 2] = held[side].astype(BF16)


def outer_rows(west, east, own, spread, rest, low, high):
    edge = (low.shape[0] + 2,) + low.shape[1:]
    return pl.pallas_call(
        edges_body,
        name="outer_rows",
        out_shape=(
            jax.ShapeDtypeStruct(own.shape, F32),
            jax.ShapeDtypeStruct(own.shape[1:], BF16),
            jax.ShapeDtypeStruct(edge, BF16),
            jax.ShapeDtypeStruct(edge, BF16),
        ),
        in_specs=[VMEM] * 7,
        out_specs=(VMEM,) * 4,
        scratch_shapes=[pltpu.VMEM((2, 2) + low.shape[1:], F32)],
        compiler_params=pltpu.CompilerParams(vmem_limit_bytes=24 << 20),
    )(west, east, own, spread, rest, low, high)


def place_body(
    odd_ref,
    arrived_ref,
    first_ref,
    adj_hbm,
    ocean_ref,
    strip_ref,
    fields_ref,
    spread_ref,
    state_ref,
    out_strip_ref,
    swap_a_ref,
    swap_b_ref,
    second_ref,
    hot,
    low,
    high,
    sems,
):
    devices = arrived_ref.shape[0]
    slots = devices * 4
    levels, rows = ocean_ref.shape[0], first_ref.shape[1]
    part = levels // 2
    late = levels - KEPT
    fetch = [
        pltpu.make_async_copy(
            adj_hbm.at[1, pl.ds(i * part, part)], second_ref.at[pl.ds(i * part, part)], sems.at[i]
        )
        for i in range(2)
    ]
    rest = pltpu.make_async_copy(
        adj_hbm.at[0, pl.ds(KEPT, late)], second_ref.at[pl.ds(levels, late)], sems.at[2]
    )
    for copy in [rest] + fetch:
        copy.start()
    last = arrived_ref[:, 2 * levels].astype(F32).reshape(slots, LANES)
    heads = last.T[120:128]
    row = fiota((rows, slots), 0)
    for c in range(2):
        found = heads[0:1] == 2.0 * row + (c + 1.0)
        hot[pl.ds(c * rows, rows), :] = jnp.where(found, 1.0, 0.0).astype(BF16)
    lane = iota((slots, LANES), 1)
    mine = west_lane((slots, LANES))
    from_west = jnp.where(mine & (lane < 120), last, 0.0).astype(BF16)
    from_east = jnp.where(mine | (lane >= 120), 0.0, last).astype(BF16)
    spread = spread_ref[...]
    strips = dot(one_hot(rows, heads[1:2] - 1.0), dot(from_west, spread).astype(BF16)) + dot(
        one_hot(rows, heads[2:3] - 1.0), dot(from_east, spread).astype(BF16)
    )
    for tile in range(STRIPS):
        out_strip_ref[tile] = strip_ref[tile].astype(F32) + strips[:, tile * LANES : (tile + 1) * LANES]
    low[...] = jnp.zeros_like(low)
    high[...] = jnp.zeros_like(high)
    wide = iota((rows, LANES), 1)

    def one(t, level):
        values = arrived_ref[:, 2 * level + t].astype(F32).reshape(slots, LANES).astype(BF16)
        k = t * levels + level
        tile, first = strip_of(k)
        ends = []
        for c in range(2):
            part = slice(c * LANES, (c + 1) * LANES)
            forced = dot(hot[pl.ds(c * rows, rows), :], values)
            before = first_ref[level, :, part] if t == 0 and level < KEPT else second_ref[level if t == 1 else levels + level - KEPT, :, part]
            total = before + forced
            ends.append(total)
            masked = total * ocean_ref[level, c].astype(F32)
            state_ref[k, c] = masked
            low[level, 3 * t : 3 * t + 3, part] = masked[0:3]
            high[level, 3 * t : 3 * t + 3, part] = masked[rows - 3 : rows]
        held = out_strip_ref[tile]
        held = jnp.where(between(wide, first + 3, first + 9), turn(ends[0], first + 3), held)
        out_strip_ref[tile] = jnp.where(
            between(wide, first + 9, first + 15), turn(ends[1], first + 15), held
        )

    for t in range(2):
        for level in range(levels):
            if t == 0 and level == KEPT:
                rest.wait()
            if t == 1 and level % part == 0:
                fetch[level // part].wait()
            one(t, level)
    for tile in range(STRIPS):
        out_strip_ref[tile] = out_strip_ref[tile] * fields_ref[2, tile]
    for out, side in ((low, slice(0, 3)), (high, slice(rows - 3, rows))):
        out[levels, 0:3, :LANES] = out_strip_ref[0, side, :]
        out[levels, 0:3, LANES:] = out_strip_ref[1, side, :]
        out[levels, 3:6, :LANES] = out_strip_ref[2, side, :]
    odd = odd_ref[0] == 1
    swap_a_ref[...] = jnp.where(odd, low[...], high[...]).astype(BF16)
    swap_b_ref[...] = jnp.where(odd, high[...], low[...]).astype(BF16)


def place_records(odd, arrived, first, adj, ocean, strip, fields, spread):
    levels, rows, cells = adj.shape[1:]
    devices = arrived.shape[0]
    edge = jax.ShapeDtypeStruct((levels + 1, 8, cells), BF16)
    return pl.pallas_call(
        place_body,
        name="place_records",
        out_shape=(
            jax.ShapeDtypeStruct((2 * levels, 2, rows, LANES), F32),
            jax.ShapeDtypeStruct((STRIPS, rows, LANES), F32),
            edge,
            edge,
        ),
        in_specs=[SMEM, VMEM, VMEM, HBM] + [VMEM] * 4,
        out_specs=(VMEM,) * 4,
        scratch_shapes=[
            pltpu.VMEM((2 * levels - KEPT, rows, cells), F32),
            pltpu.VMEM((2 * rows, devices * 4), BF16),
            pltpu.VMEM(edge.shape, F32),
            pltpu.VMEM(edge.shape, F32),
            pltpu.SemaphoreType.DMA((3,)),
        ],
        compiler_params=pltpu.CompilerParams(vmem_limit_bytes=24 << 20),
    )(odd, arrived, first, hbm(adj), ocean, strip, fields, spread)


def steps_body(
    where_ref,
    spread_ref,
    state_ref,
    strip_ref,
    swap_a_ref,
    swap_b_ref,
    ef_hbm,
    nf_hbm,
    ocean_ref,
    fields_ref,
    low_ref,
    high_ref,
    out_ref,
    flow_all,
    ocean,
    strip_flow,
    strip_ocean,
    coef,
    cells_a,
    cells_b,
    cells_c,
    patch,
    below,
    above,
    rows_low,
    rows_high,
    done,
    sems,
    level_sems,
):
    levels, rows = ocean_ref.shape[0], ocean_ref.shape[2]

    groups = ((0, 2), (2, levels))

    def arrivals(group):
        first, end = groups[group]
        span = pl.ds(first, end - first)
        return [
            pltpu.make_async_copy(
                source.at[span, :, pl.ds(x * LANES, LANES)],
                flow_all.at[span, f, x, pl.ds(16, rows), :],
                level_sems.at[2 * f + x, group],
            )
            for f, source in enumerate((ef_hbm, nf_hbm))
            for x in range(2)
        ]

    for group in range(2):
        for copy in arrivals(group):
            copy.start()
    tall = rows + 16
    inner = slice(16, 16 + rows)
    before, after = slice(13, 16), slice(16 + rows, 19 + rows)
    at_start, at_end, odd = where_ref[0], where_ref[1], where_ref[2] == 1
    lane, sub = iota((8, LANES), 1), iota((8, LANES), 0)
    for ref in (strip_flow.at[0], strip_flow.at[1], strip_ocean):
        ref[0, 0:16] = jnp.zeros((16, LANES), F32)
        ref[0, 16 + rows : 32 + rows] = jnp.zeros((16, LANES), F32)
    for x in range(2):
        ocean[x, 0:16] = jnp.zeros((16, LANES), F32)
        ocean[x, 16 + rows : 32 + rows] = jnp.zeros((16, LANES), F32)
    for ref in (cells_a, cells_b, cells_c):
        for t in range(2):
            for x in range(2):
                ref[t, x, 0:16] = jnp.zeros((16, LANES), F32)
                ref[t, x, 16 + rows : 32 + rows] = jnp.zeros((16, LANES), F32)
    below[...] = jnp.where(odd, swap_a_ref[...].astype(F32), swap_b_ref[...].astype(F32))
    above[...] = jnp.where(odd, swap_b_ref[...].astype(F32), swap_a_ref[...].astype(F32))
    rows_low[...] = low_ref[...].astype(F32)
    rows_high[...] = high_ref[...].astype(F32)
    top = 8 + rows
    shut_s = (sub == 0) & (at_start == 1)
    shut_n = (sub == 7) & (at_end == 1)

    def close_top(ref):
        ref[top : top + 8] = jnp.where(shut_n, 0.0, ref[top : top + 8])

    def prepare(x, i, flow, here, turned):
        at = slice(8 * i, 8 * i + 8)
        ce = jnp.maximum(here, 0.0)
        cw = -jnp.minimum(turned, 0.0)
        cn = jnp.maximum(flow[1, x, at], 0.0)
        cs = -jnp.minimum(flow[1, x, 8 * i - 1 : 8 * i + 7], 0.0)
        coef[0, x, at] = ce
        coef[1, x, at] = cw
        coef[2, x, at] = cn
        coef[3, x, at] = cs
        coef[4, x, at] = 1.0 - ce - cw - cn - cs

    def around_k(i, k):
        total = 4.0 * k
        if i == 2:
            total = total - jnp.where(shut_s, k, 0.0)
        if i == 1 + rows // 8:
            total = total - jnp.where(shut_n, k, 0.0)
        return total

    def update(source, x, i, k, here, east, west):
        at = slice(8 * i, 8 * i + 8)
        north = source[x, 8 * i + 1 : 8 * i + 9]
        south = source[x, 8 * i - 1 : 8 * i + 7]
        return (
            (coef[4, x, at] - around_k(i, k)) * here
            + (coef[0, x, at] + k) * east
            + (coef[1, x, at] + k) * west
            + (coef[2, x, at] + k) * north
            + (coef[3, x, at] + k) * south
        )

    def tiles(step):
        edge = 1 if step == STEPS - 1 else 0
        return range(1 + edge, 1 + tall // 8 - edge)

    for tile in range(STRIPS):
        k = jnp.zeros((1, LANES), F32)
        for s in range(7):
            slice_id = 7 * tile + s
            if slice_id < 2 * levels:
                own = between(iota((1, LANES), 1), 18 * s, 18 * s + 18)
                k = jnp.where(own, spread_ref[slice_id // levels, slice_id % levels], k)
        block = levels + tile // 2
        part = slice((tile % 2) * LANES, (tile % 2 + 1) * LANES)
        for f, dest in enumerate((strip_flow.at[0, 0], strip_flow.at[1, 0], strip_ocean.at[0])):
            dest[before] = rows_low[block, 3 * f : 3 * f + 3, part]
            dest[inner] = fields_ref[f, tile]
            dest[after] = rows_high[block, 3 * f : 3 * f + 3, part]
        close_top(strip_flow.at[1, 0])
        for i in range(1, 1 + tall // 8):
            face = strip_flow[0, 0, 8 * i : 8 * i + 8]
            prepare(0, i, strip_flow, face, pltpu.roll(face, 1, 1))
        here = slice(3 * (tile // 2), 3 * (tile // 2) + 3)
        cells_a[0, 0, before] = below[levels, here, part]
        cells_a[0, 0, inner] = strip_ref[tile]
        cells_a[0, 0, after] = above[levels, here, part]
        source = cells_a.at[0]
        for step in range(STEPS):
            dest = (cells_b, cells_c, None)[step]
            for i in tiles(step):
                at = slice(8 * i, 8 * i + 8)
                value = source[0, at]
                total = update(
                    source, 0, i, k, value, pltpu.roll(value, LANES - 1, 1), pltpu.roll(value, 1, 1)
                )
                if dest is None:
                    patch[tile, 8 * i - 16 : 8 * i - 8] = total
                else:
                    dest[0, 0, at] = total * strip_ocean[0, at]
            source = dest.at[0] if dest is not None else None

    def leave(level):
        return pltpu.make_async_copy(done.at[:, level], out_ref.at[:, level], sems.at[level])

    def one(level, carry):
        flow = flow_all.at[level]
        for group in range(2):

            @pl.when(level == groups[group][0])
            def _():
                for copy in arrivals(group):
                    copy.wait()

        for f in range(2):
            for x in range(2):
                flow[f, x, 0:16] = jnp.zeros((16, LANES), F32)
                flow[f, x, 16 + rows : 32 + rows] = jnp.zeros((16, LANES), F32)
        for x in range(2):
            part = slice(x * LANES, (x + 1) * LANES)
            ocean[x, inner] = ocean_ref[level, x].astype(F32)
            for f, dest in enumerate((flow.at[0, x], flow.at[1, x], ocean.at[x])):
                dest[before] = rows_low[level, 3 * f : 3 * f + 3, part]
                dest[after] = rows_high[level, 3 * f : 3 * f + 3, part]
            close_top(flow.at[1, x])
            for t in range(2):
                cells_a[t, x, before] = below[level, 3 * t : 3 * t + 3, part]
                cells_a[t, x, inner] = state_ref[t * levels + level, x]
                cells_a[t, x, after] = above[level, 3 * t : 3 * t + 3, part]
        for i in range(1, 1 + tall // 8):
            at = slice(8 * i, 8 * i + 8)
            faces = [flow[0, x, at] for x in range(2)]
            turned = [pltpu.roll(v, 1, 1) for v in faces]
            turned[1] = jnp.where(lane == 0, turned[0], turned[1])
            for x in range(2):
                prepare(x, i, flow, faces[x], turned[x])
        ks = [spread_ref[t, level] for t in range(2)]
        spots = [strip_of(t * levels + level) for t in range(2)]
        buffers = (cells_a, cells_b, cells_c)
        for step in range(STEPS):
            for i in tiles(step):
                at = slice(8 * i, 8 * i + 8)
                for t in range(2):
                    source = buffers[step].at[t]
                    here = [source[x, at] for x in range(2)]
                    right = [pltpu.roll(v, LANES - 1, 1) for v in here]
                    left = [pltpu.roll(v, 1, 1) for v in here]
                    east = [jnp.where(lane == LANES - 1, right[1], right[0]), right[1]]
                    west = [left[0], jnp.where(lane == 0, left[0], left[1])]
                    for x in range(2):
                        total = update(source, x, i, ks[t], here[x], east[x], west[x])
                        if step < STEPS - 1:
                            buffers[step + 1][t, x, at] = total * ocean[x, at]
                            continue
                        tile, first = spots[t]
                        shift, keep = (125 - first, lane < 3) if x == 0 else (113 - first, lane >= 125)
                        fixed = turn(patch[tile, 8 * i - 16 : 8 * i - 8], shift)
                        done[t, level, 8 * i - 16 : 8 * i - 8, x * LANES : (x + 1) * LANES] = (
                            jnp.where(keep, fixed, total)
                        )
        leave(level).start()
        return carry

    lax.fori_loop(0, levels, one, 0)
    for level in range(levels):
        leave(level).wait()


def run_steps(where, spread, state, strip, swap_a, swap_b, ef, nf, ocean, fields, low, high):
    levels, rows = ocean.shape[0], ocean.shape[2]
    tall, width = rows + 32, 2 * LANES
    buffer = pltpu.VMEM((2, 2, tall, LANES), F32)
    return pl.pallas_call(
        steps_body,
        name="three_steps",
        out_shape=jax.ShapeDtypeStruct((2, levels, rows, width), F32),
        in_specs=[SMEM, SMEM] + [VMEM] * 4 + [HBM] * 2 + [VMEM] * 4,
        out_specs=HBM,
        scratch_shapes=[
            pltpu.VMEM((levels, 2, 2, tall, LANES), F32),
            pltpu.VMEM((2, tall, LANES), F32),
            pltpu.VMEM((2, 1, tall, LANES), F32),
            pltpu.VMEM((1, tall, LANES), F32),
            pltpu.VMEM((5, 2, tall, LANES), F32),
            buffer,
            buffer,
            buffer,
            pltpu.VMEM((STRIPS, rows, LANES), F32),
            pltpu.VMEM(swap_a.shape, F32),
            pltpu.VMEM(swap_a.shape, F32),
            pltpu.VMEM(low.shape, F32),
            pltpu.VMEM(low.shape, F32),
            pltpu.VMEM((2, levels, rows, width), F32),
            pltpu.SemaphoreType.DMA((levels,)),
            pltpu.SemaphoreType.DMA((4, 2)),
        ],
        compiler_params=pltpu.CompilerParams(vmem_limit_bytes=24 << 20),
    )(where, spread, state, strip, swap_a, swap_b, hbm(ef), hbm(nf), ocean, fields, low, high)


def around(block, axis, distance):
    count = lax.axis_size(axis)
    return lax.ppermute(block, axis, [(i, (i + distance) % count) for i in range(count)])


def along(block, axis, distance):
    count = lax.axis_size(axis)
    route = [(i, i + distance) for i in range(count) if 0 <= i + distance < count]
    return lax.ppermute(block, axis, route)


def swapped(block, axis, start):
    count = lax.axis_size(axis)
    lower = range(start, count - 1, 2)
    return lax.ppermute(block, axis, [(i, i + 1) for i in lower] + [(i + 1, i) for i in lower])


def per_device(
    adjoint_in,
    east_flow,
    north_flow,
    diffusivity,
    land_mask,
    forcing,
    obs_tile,
    obs_block,
    obs_live,
):
    n_lat, n_lon = lax.axis_size("lat"), lax.axis_size("lon")
    lat = lax.axis_index("lat")
    odd = lat % 2
    where = jnp.stack([lat == 0, lat == n_lat - 1, odd == 1]).astype(jnp.int32)
    flat = forcing.transpose(0, 1, 3, 2, 4).reshape(-1, forcing.shape[4])
    packed = pack_records(flat, obs_tile, obs_block, obs_live, n_lat * n_lon, n_lon)
    arrived = lax.all_to_all(packed, ("lat", "lon"), split_axis=0, concat_axis=0, tiled=True)
    columns, ocean = outer_columns(adjoint_in, east_flow, north_flow, land_mask)
    west = around(columns, "lon", 1)
    east = around(columns, "lon", -1)
    own, spread, rest, adj_first, low, high = own_strips(
        east_flow, north_flow, adjoint_in, ocean
    )
    fields, adj_strip, low, high = outer_rows(west, east, own, spread, rest, low, high)
    below = along(high, "lat", 1)
    above = along(low, "lat", -1)
    state, strip, swap_a, swap_b = place_records(
        odd.reshape(1).astype(jnp.int32), arrived, adj_first, adjoint_in, ocean, adj_strip, fields, spread
    )
    swap_a = swapped(swap_a, "lat", 0)
    swap_b = swapped(swap_b, "lat", 1)
    return run_steps(
        where,
        diffusivity,
        state,
        strip,
        swap_a,
        swap_b,
        east_flow,
        north_flow,
        ocean,
        fields,
        below,
        above,
    )


def solution(mesh):
    in_specs = (
        P(None, None, "lat", "lon"),
        P(None, "lat", "lon"),
        P(None, "lat", "lon"),
        P(),
        P(None, "lat", "lon"),
        P(("lat", "lon"), None, None, None, None),
        P(("lat", "lon"), None),
        P(("lat", "lon"), None),
        P(("lat", "lon")),
    )
    out_specs = P(None, None, "lat", "lon")
    return jax.shard_map(
        per_device, mesh=mesh, in_specs=in_specs, out_specs=out_specs, check_vma=False
    )
```

```python
import functools

import jax
import jax.numpy as jnp
from jax import lax
from jax.experimental import pallas as pl
from jax.experimental.pallas import tpu as pltpu
from jax.sharding import PartitionSpec as P

STEPS = 3
LANES = 128
KEPT = 9
F32 = jnp.float32
BF16 = jnp.bfloat16
HBM = pl.BlockSpec(memory_space=pltpu.HBM)
VMEM = pl.BlockSpec(memory_space=pltpu.VMEM)
SMEM = pl.BlockSpec(memory_space=pltpu.SMEM)


def iota(shape, dim):
    return lax.broadcasted_iota(jnp.int32, shape, dim)


def fiota(shape, dim):
    return iota(shape, dim).astype(F32)


def west_lane(shape):
    lane = fiota(shape, 1)
    return lane - 6.0 * jnp.floor((lane + 0.5) / 6.0) < 3.0


def one_hot(rows, code):
    shape = (rows, code.shape[1])
    return jnp.where(fiota(shape, 0) == code, 1.0, 0.0).astype(BF16)


def dot(a, b):
    return jnp.dot(a, b, preferred_element_type=F32)


def pack_body(
    n_lon, live_ref, tile_in, block_in, forcing_in, out_hbm,
    tile_ref, block_ref, forcing_ref, out_ref, wide, sems, out_sems,
):
    records, devices = tile_ref.shape[1], out_ref.shape[0]
    count = forcing_ref.shape[0] // records
    levels = count // 2
    moves = [
        pltpu.make_async_copy(source, dest, sems.at[i])
        for i, (source, dest) in enumerate(
            (
                (tile_in, tile_ref),
                (block_in, block_ref),
                (forcing_in, forcing_ref),
            )
        )
    ]
    for move in moves:
        move.start()
    for move in moves[:2]:
        move.wait()
    tile = tile_ref[...].astype(F32)
    block = block_ref[...].astype(F32)
    square = (records, records)
    low, high = iota(square, 0), iota(square, 1)
    tile_col = jnp.sum(jnp.where(low == high, tile, 0.0), axis=1, keepdims=True)
    block_col = jnp.sum(jnp.where(low == high, block, 0.0), axis=1, keepdims=True)
    earlier = jnp.where((tile_col == tile) & (low < high), 1.0, 0.0)
    rank = jnp.sum(earlier, axis=0, keepdims=True)
    live = iota((1, records), 1) < live_ref[0]
    band = jnp.floor((tile + 0.5) / n_lon) * n_lon
    column = tile - band
    east = band + jnp.where(column == n_lon - 1, 0.0, column + 1.0)
    west = band + jnp.where(column == 0.0, n_lon - 1.0, column - 1.0)
    half = block - 2.0 * jnp.floor(block * 0.5)
    code = jnp.where(live, tile * 4.0 + rank, -8.0)
    to_east = jnp.where(live & (half == 1.0), east * 4.0 + rank, -8.0)
    to_west = jnp.where(live & (half == 0.0), west * 4.0 + rank, -8.0)
    moves[2].wait()
    wide[...] = forcing_ref[...].astype(F32)
    sent = []

    def send(q, values):
        out_ref[:, q] = values.astype(BF16).reshape(devices, 4, LANES)
        if q % 2 == 1 or q == count:
            span = pl.ds(q, 1) if q == count else pl.ds(q - 1, 2)
            copy = pltpu.make_async_copy(
                out_ref.at[:, span], out_hbm.at[:, span], out_sems.at[q // 2]
            )
            copy.start()
            sent.append(copy)

    first = one_hot(devices * 4, code)
    lane = iota((records, LANES), 1)
    edges = jnp.zeros((records, LANES), F32)
    for place in range(count):
        level, t = divmod(place, 2)
        k = t * levels + level
        values = wide[pl.ds(place, records, stride=count), :]
        turned = pltpu.roll(values, (6 * k + 3) % LANES, 1)
        edges = jnp.where((lane >= 6 * k) & (lane < 6 * k + 6), turned, edges)
        send(place, dot(first, values.astype(BF16)))
    row_col = jnp.floor(block_col * 0.5) + 1.0
    mine = west_lane((records, LANES))
    data = lane < 6 * count
    from_west = jnp.where(data, jnp.where(mine, edges, 0.0), jnp.where(lane == 121, row_col, 0.0))
    from_east = jnp.where(data, jnp.where(mine, 0.0, edges), jnp.where(lane == 122, row_col, 0.0))
    header = jnp.where(lane == 120, block_col + 1.0, 0.0)
    last = (
        dot(first, header.astype(BF16))
        + dot(one_hot(devices * 4, to_east), from_west.astype(BF16))
        + dot(one_hot(devices * 4, to_west), from_east.astype(BF16))
    )
    send(count, last)
    for copy in sent:
        copy.wait()


def pack_records(forcing, tile, block, live, devices, n_lon):
    records, width = tile.shape[1], forcing.shape[1]
    levels = forcing.shape[0] // records // 2
    out = (devices, 2 * levels + 1, 4, width)
    return pl.pallas_call(
        functools.partial(pack_body, n_lon),
        name="pack_records",
        out_shape=pltpu.HBM(out, BF16),
        in_specs=[SMEM] + [HBM] * 3,
        out_specs=HBM,
        scratch_shapes=[
            pltpu.VMEM(tile.shape, jnp.int32),
            pltpu.VMEM(block.shape, jnp.int32),
            pltpu.VMEM(forcing.shape, BF16),
            pltpu.VMEM(out, BF16),
            pltpu.VMEM(forcing.shape, F32),
            pltpu.SemaphoreType.DMA((3,)),
            pltpu.SemaphoreType.DMA((levels + 1,)),
        ],
        compiler_params=pltpu.CompilerParams(vmem_limit_bytes=24 << 20),
    )(live, *map(hbm, (tile, block, forcing)))


STRIPS = 3


def strip_of(k):
    return k // 7, 18 * lax.rem(k, 7) if not isinstance(k, int) else 18 * (k % 7)


def turn(values, shift):
    if isinstance(shift, int):
        return pltpu.roll(values, shift % LANES, 1)
    return pltpu.roll(values, lax.rem(shift + 4 * LANES, LANES), 1)


def hbm(x):
    return pltpu.with_memory_space_constraint(x, pltpu.HBM)


def between(lane, low, high):
    return (lane >= low) & (lane < high)


def columns_body(
    adj_hbm, ef_hbm, nf_hbm, mask_hbm, out_ref, ocean_ref, adj_ref, flow_ref, mask, held, sems
):
    levels, rows = mask.shape[0], mask.shape[1]

    def moves(level):
        pairs = [(mask_hbm.at[level], mask.at[level])]
        pairs += [(adj_hbm.at[t, level], adj_ref.at[t, level]) for t in range(2)]
        pairs += [
            (
                source.at[level, :, pl.ds(x * LANES, LANES)],
                flow_ref.at[level, f, x],
            )
            for f, source in enumerate((ef_hbm, nf_hbm))
            for x in range(2)
        ]
        return [
            pltpu.make_async_copy(source, dest, sems.at[i, level])
            for i, (source, dest) in enumerate(pairs)
        ]

    for level in range(levels):
        for copy in moves(level):
            copy.start()
    lane = iota((rows, LANES), 1)
    held[...] = jnp.zeros_like(held)

    def put(tile, place, first, second):
        ends = jnp.where(lane < 64, first, second)
        inside = between(lane, 6 * place, 6 * place + 6)
        held[tile] = jnp.where(inside, turn(ends, 6 * place + 3), held[tile])

    def one(level, carry):
        for copy in moves(level):
            copy.wait()
        for x in range(2):
            ocean_ref[level, x] = mask[level, :, x * LANES : (x + 1) * LANES].astype(F32).astype(BF16)
        for t in range(2):
            put(0, t * levels + level, adj_ref[t, level, :, :LANES], adj_ref[t, level, :, LANES:])
        put(1, level, flow_ref[level, 0, 0], flow_ref[level, 0, 1])
        put(1, levels + level, flow_ref[level, 1, 0], flow_ref[level, 1, 1])
        put(2, level, mask[level, :, :LANES].astype(F32), mask[level, :, LANES:].astype(F32))
        return carry

    lax.fori_loop(0, levels, one, 0)
    for tile in range(3):
        out_ref[:, tile * LANES : (tile + 1) * LANES] = held[tile].astype(BF16)


def outer_columns(adj, ef, nf, mask):
    levels, rows, cells = ef.shape
    return pl.pallas_call(
        columns_body,
        name="outer_columns",
        out_shape=(
            jax.ShapeDtypeStruct((rows, 3 * LANES), BF16),
            jax.ShapeDtypeStruct((levels, 2, rows, LANES), BF16),
        ),
        in_specs=[HBM] * 4,
        out_specs=(VMEM,) * 2,
        scratch_shapes=[
            pltpu.VMEM(adj.shape, F32),
            pltpu.VMEM((levels, 2, 2, rows, LANES), F32),
            pltpu.VMEM(mask.shape, jnp.int32),
            pltpu.VMEM((3, rows, LANES), F32),
            pltpu.SemaphoreType.DMA((7, levels)),
        ],
        compiler_params=pltpu.CompilerParams(vmem_limit_bytes=24 << 20),
    )(*map(hbm, (adj, ef, nf, mask)))


def own_body(
    ef_hbm, nf_hbm, adj_hbm, ocean_ref,
    strips, spread_ref, rest_ref, first_ref, low_out, high_out,
    flow_ref, low, high, sems, adj_sem,
):
    levels, rows = ocean_ref.shape[0], ocean_ref.shape[2]

    def moves(level):
        return [
            pltpu.make_async_copy(
                source.at[level, :, pl.ds(x * LANES, LANES)],
                flow_ref.at[level, f, x],
                sems.at[2 * f + x, level],
            )
            for f, source in enumerate((ef_hbm, nf_hbm))
            for x in range(2)
        ]

    for level in range(levels):
        for copy in moves(level):
            copy.start()
    fetch = pltpu.make_async_copy(adj_hbm.at[0, pl.ds(0, KEPT)], first_ref, adj_sem)
    fetch.start()
    source, target = fiota((LANES, LANES), 0), fiota((1, LANES), 1)
    order = jnp.floor((target + 0.5) / 18.0)
    offset = target - 18.0 * order
    inner = jnp.where(offset < 3.0, offset, offset - 12.0)
    used = ((offset < 3.0) | (offset >= 15.0)) & (order < 7.0)
    for tile in range(STRIPS):
        k = order + 7.0 * tile
        level = jnp.where(k < levels, k, k - levels)
        live = used & (k < 2.0 * levels)
        for m, place in enumerate((k, level, level + levels)):
            hit = source == jnp.where(live, 6.0 * place + inner, -1.0)
            part = slice(tile * LANES, (tile + 1) * LANES)
            ones = jnp.where(hit, 1.0, 0.0).astype(BF16)
            if m == 0:
                spread_ref[:, part] = ones
            else:
                rest_ref[m - 1, :, part] = ones
    strips[...] = jnp.zeros_like(strips)
    low[...] = jnp.zeros_like(low)
    high[...] = jnp.zeros_like(high)
    lane = iota((rows, LANES), 1)

    def one(level, carry):
        for copy in moves(level):
            copy.wait()
        for f, ref in enumerate((flow_ref.at[level, 0], flow_ref.at[level, 1], ocean_ref.at[level])):
            ends = [ref[x].astype(F32) for x in range(2)]
            for x in range(2):
                here = slice(x * LANES, (x + 1) * LANES)
                low[level, 3 * f : 3 * f + 3, here] = ends[x][0:3]
                high[level, 3 * f : 3 * f + 3, here] = ends[x][rows - 3 : rows]
            own = jnp.where(lane < 9, turn(ends[0], 3), turn(ends[1], 15))
            for t in range(2):
                tile, first = strip_of(t * levels + level)
                keep = between(lane, first + 3, first + 15)
                strips[f, tile] = jnp.where(keep, turn(own, first), strips[f, tile])
        return carry

    for level in range(levels):
        one(level, 0)
    low_out[...] = low[...].astype(BF16)
    high_out[...] = high[...].astype(BF16)
    fetch.wait()


def own_strips(ef, nf, adj, ocean):
    levels, rows = ef.shape[0], ef.shape[1]
    return pl.pallas_call(
        own_body,
        name="own_strips",
        out_shape=(
            jax.ShapeDtypeStruct((3, STRIPS, rows, LANES), F32),
            jax.ShapeDtypeStruct((LANES, STRIPS * LANES), BF16),
            jax.ShapeDtypeStruct((2, LANES, STRIPS * LANES), BF16),
            jax.ShapeDtypeStruct((KEPT,) + adj.shape[2:], F32),
            jax.ShapeDtypeStruct((levels, 16, 2 * LANES), BF16),
            jax.ShapeDtypeStruct((levels, 16, 2 * LANES), BF16),
        ),
        in_specs=[HBM, HBM, HBM, VMEM],
        out_specs=(VMEM,) * 6,
        scratch_shapes=[
            pltpu.VMEM((levels, 2, 2, rows, LANES), F32),
            pltpu.VMEM((levels, 16, 2 * LANES), F32),
            pltpu.VMEM((levels, 16, 2 * LANES), F32),
            pltpu.SemaphoreType.DMA((4, levels)),
            pltpu.SemaphoreType.DMA,
        ],
        cost_estimate=pl.CostEstimate(flops=10**8, bytes_accessed=10**7, transcendentals=0),
        compiler_params=pltpu.CompilerParams(vmem_limit_bytes=24 << 20),
    )(hbm(ef), hbm(nf), hbm(adj), ocean)


def edges_body(
    odd_ref, west, east, own_ref, spread_ref, rest_ref, low_main, high_main,
    strips, adj, swap_a, swap_b, held,
):
    levels, rows = low_main.shape[0], own_ref.shape[2]

    def halo(tile, m):
        part = slice(tile * LANES, (tile + 1) * LANES)
        theirs, ours = west[:, part].astype(F32), east[:, part].astype(F32)
        merged = jnp.where(west_lane(theirs.shape), theirs, ours).astype(BF16)
        return dot(merged, rest_ref[m - 1] if m else spread_ref[...])

    for f, (source, m) in enumerate(((1, 1), (1, 2), (2, 1))):
        halos = halo(source, m)
        for tile in range(STRIPS):
            strips[f, tile] = own_ref[f, tile] + halos[:, tile * LANES : (tile + 1) * LANES]
    halos = halo(0, 0)
    for tile in range(STRIPS):
        adj[tile] = halos[:, tile * LANES : (tile + 1) * LANES].astype(BF16)
    held[...] = jnp.zeros_like(held)
    for side, first in enumerate((0, rows - 3)):
        at = slice(first, first + 3)
        for f in range(3):
            here = slice(3 * f, 3 * f + 3)
            held[side, 0, here, :LANES] = strips[f, 0, at, :]
            held[side, 0, here, LANES:] = strips[f, 1, at, :]
            held[side, 1, here, :LANES] = strips[f, 2, at, :]
    odd = odd_ref[0] == 1
    low, high = low_main[...].astype(F32), high_main[...].astype(F32)
    swap_a[0:levels] = jnp.where(odd, low, high).astype(BF16)
    swap_b[0:levels] = jnp.where(odd, high, low).astype(BF16)
    swap_a[levels : levels + 2] = jnp.where(odd, held[0], held[1]).astype(BF16)
    swap_b[levels : levels + 2] = jnp.where(odd, held[1], held[0]).astype(BF16)


def outer_rows(odd, west, east, own, spread, rest, low, high):
    edge = (low.shape[0] + 2,) + low.shape[1:]
    return pl.pallas_call(
        edges_body,
        name="outer_rows",
        out_shape=(
            jax.ShapeDtypeStruct(own.shape, F32),
            jax.ShapeDtypeStruct(own.shape[1:], BF16),
            jax.ShapeDtypeStruct(edge, BF16),
            jax.ShapeDtypeStruct(edge, BF16),
        ),
        in_specs=[SMEM] + [VMEM] * 7,
        out_specs=(VMEM,) * 4,
        scratch_shapes=[pltpu.VMEM((2, 2) + low.shape[1:], F32)],
        compiler_params=pltpu.CompilerParams(vmem_limit_bytes=24 << 20),
    )(odd, west, east, own, spread, rest, low, high)


def place_body(
    odd_ref,
    arrived_ref,
    first_ref,
    adj_hbm,
    ocean_ref,
    strip_ref,
    fields_ref,
    spread_ref,
    state_ref,
    out_strip_ref,
    swap_a_ref,
    swap_b_ref,
    second_ref,
    hot,
    low,
    high,
    sems,
):
    devices = arrived_ref.shape[0]
    slots = devices * 4
    levels, rows = ocean_ref.shape[0], first_ref.shape[1]
    part = levels // 2
    late = levels - KEPT
    fetch = [
        pltpu.make_async_copy(
            adj_hbm.at[1, pl.ds(i * part, part)], second_ref.at[pl.ds(i * part, part)], sems.at[i]
        )
        for i in range(2)
    ]
    rest = pltpu.make_async_copy(
        adj_hbm.at[0, pl.ds(KEPT, late)], second_ref.at[pl.ds(levels, late)], sems.at[2]
    )
    for copy in [rest] + fetch:
        copy.start()
    last = arrived_ref[:, 2 * levels].astype(F32).reshape(slots, LANES)
    heads = last.T[120:128]
    row = fiota((rows, slots), 0)
    for c in range(2):
        found = heads[0:1] == 2.0 * row + (c + 1.0)
        hot[pl.ds(c * rows, rows), :] = jnp.where(found, 1.0, 0.0).astype(BF16)
    lane = iota((slots, LANES), 1)
    mine = west_lane((slots, LANES))
    from_west = jnp.where(mine & (lane < 120), last, 0.0).astype(BF16)
    from_east = jnp.where(mine | (lane >= 120), 0.0, last).astype(BF16)
    spread = spread_ref[...]
    strips = dot(one_hot(rows, heads[1:2] - 1.0), dot(from_west, spread).astype(BF16)) + dot(
        one_hot(rows, heads[2:3] - 1.0), dot(from_east, spread).astype(BF16)
    )
    for tile in range(STRIPS):
        out_strip_ref[tile] = strip_ref[tile].astype(F32) + strips[:, tile * LANES : (tile + 1) * LANES]
    low[...] = jnp.zeros_like(low)
    high[...] = jnp.zeros_like(high)
    wide = iota((rows, LANES), 1)

    def one(t, level):
        values = arrived_ref[:, 2 * level + t].astype(F32).reshape(slots, LANES).astype(BF16)
        k = t * levels + level
        tile, first = strip_of(k)
        ends = []
        for c in range(2):
            part = slice(c * LANES, (c + 1) * LANES)
            forced = dot(hot[pl.ds(c * rows, rows), :], values)
            before = first_ref[level, :, part] if t == 0 and level < KEPT else second_ref[level if t == 1 else levels + level - KEPT, :, part]
            total = before + forced
            ends.append(total)
            masked = total * ocean_ref[level, c].astype(F32)
            state_ref[k, c] = masked
            low[level, 3 * t : 3 * t + 3, part] = masked[0:3]
            high[level, 3 * t : 3 * t + 3, part] = masked[rows - 3 : rows]
        held = out_strip_ref[tile]
        held = jnp.where(between(wide, first + 3, first + 9), turn(ends[0], first + 3), held)
        out_strip_ref[tile] = jnp.where(
            between(wide, first + 9, first + 15), turn(ends[1], first + 15), held
        )

    for t in range(2):
        for level in range(levels):
            if t == 0 and level == KEPT:
                rest.wait()
            if t == 1 and level % part == 0:
                fetch[level // part].wait()
            one(t, level)
    for tile in range(STRIPS):
        out_strip_ref[tile] = out_strip_ref[tile] * fields_ref[2, tile]
    for out, side in ((low, slice(0, 3)), (high, slice(rows - 3, rows))):
        out[levels, 0:3, :LANES] = out_strip_ref[0, side, :]
        out[levels, 0:3, LANES:] = out_strip_ref[1, side, :]
        out[levels, 3:6, :LANES] = out_strip_ref[2, side, :]
    odd = odd_ref[0] == 1
    swap_a_ref[...] = jnp.where(odd, low[...], high[...]).astype(BF16)
    swap_b_ref[...] = jnp.where(odd, high[...], low[...]).astype(BF16)


def place_records(odd, arrived, first, adj, ocean, strip, fields, spread):
    levels, rows, cells = adj.shape[1:]
    devices = arrived.shape[0]
    edge = jax.ShapeDtypeStruct((levels + 1, 8, cells), BF16)
    return pl.pallas_call(
        place_body,
        name="place_records",
        out_shape=(
            jax.ShapeDtypeStruct((2 * levels, 2, rows, LANES), F32),
            jax.ShapeDtypeStruct((STRIPS, rows, LANES), F32),
            edge,
            edge,
        ),
        in_specs=[SMEM, VMEM, VMEM, HBM] + [VMEM] * 4,
        out_specs=(VMEM,) * 4,
        scratch_shapes=[
            pltpu.VMEM((2 * levels - KEPT, rows, cells), F32),
            pltpu.VMEM((2 * rows, devices * 4), BF16),
            pltpu.VMEM(edge.shape, F32),
            pltpu.VMEM(edge.shape, F32),
            pltpu.SemaphoreType.DMA((3,)),
        ],
        compiler_params=pltpu.CompilerParams(vmem_limit_bytes=24 << 20),
    )(odd, arrived, first, hbm(adj), ocean, strip, fields, spread)


def steps_body(
    where_ref,
    spread_ref,
    state_ref,
    strip_ref,
    swap_a_ref,
    swap_b_ref,
    ef_hbm,
    nf_hbm,
    ocean_ref,
    fields_ref,
    low_ref,
    high_ref,
    out_ref,
    flow_all,
    ocean,
    strip_flow,
    strip_ocean,
    coef,
    cells_a,
    cells_b,
    cells_c,
    patch,
    below,
    above,
    rows_low,
    rows_high,
    done,
    sems,
    level_sems,
):
    levels, rows = ocean_ref.shape[0], ocean_ref.shape[2]

    groups = ((0, 2), (2, levels))

    def arrivals(group):
        first, end = groups[group]
        span = pl.ds(first, end - first)
        return [
            pltpu.make_async_copy(
                source.at[span, :, pl.ds(x * LANES, LANES)],
                flow_all.at[span, f, x, pl.ds(16, rows), :],
                level_sems.at[2 * f + x, group],
            )
            for f, source in enumerate((ef_hbm, nf_hbm))
            for x in range(2)
        ]

    for group in range(2):
        for copy in arrivals(group):
            copy.start()
    tall = rows + 16
    inner = slice(16, 16 + rows)
    before, after = slice(13, 16), slice(16 + rows, 19 + rows)
    at_start, at_end, odd = where_ref[0], where_ref[1], where_ref[2] == 1
    lane, sub = iota((8, LANES), 1), iota((8, LANES), 0)
    for ref in (strip_flow.at[0], strip_flow.at[1], strip_ocean):
        ref[0, 0:16] = jnp.zeros((16, LANES), F32)
        ref[0, 16 + rows : 32 + rows] = jnp.zeros((16, LANES), F32)
    for x in range(2):
        ocean[x, 0:16] = jnp.zeros((16, LANES), F32)
        ocean[x, 16 + rows : 32 + rows] = jnp.zeros((16, LANES), F32)
    for ref in (cells_a, cells_b, cells_c):
        for t in range(2):
            for x in range(2):
                ref[t, x, 0:16] = jnp.zeros((16, LANES), F32)
                ref[t, x, 16 + rows : 32 + rows] = jnp.zeros((16, LANES), F32)
    below[...] = jnp.where(odd, swap_a_ref[...].astype(F32), swap_b_ref[...].astype(F32))
    above[...] = jnp.where(odd, swap_b_ref[...].astype(F32), swap_a_ref[...].astype(F32))
    edge_a, edge_b = low_ref[...].astype(F32), high_ref[...].astype(F32)
    rows_low[...] = jnp.where(odd, edge_a, edge_b)
    rows_high[...] = jnp.where(odd, edge_b, edge_a)
    top = 8 + rows
    shut_s = (sub == 0) & (at_start == 1)
    shut_n = (sub == 7) & (at_end == 1)

    def close_top(ref):
        ref[top : top + 8] = jnp.where(shut_n, 0.0, ref[top : top + 8])

    def prepare(x, i, flow, here, turned):
        at = slice(8 * i, 8 * i + 8)
        ce = jnp.maximum(here, 0.0)
        cw = -jnp.minimum(turned, 0.0)
        cn = jnp.maximum(flow[1, x, at], 0.0)
        cs = -jnp.minimum(flow[1, x, 8 * i - 1 : 8 * i + 7], 0.0)
        coef[0, x, at] = ce
        coef[1, x, at] = cw
        coef[2, x, at] = cn
        coef[3, x, at] = cs
        coef[4, x, at] = 1.0 - ce - cw - cn - cs

    def around_k(i, k):
        total = 4.0 * k
        if i == 2:
            total = total - jnp.where(shut_s, k, 0.0)
        if i == 1 + rows // 8:
            total = total - jnp.where(shut_n, k, 0.0)
        return total

    def update(source, x, i, k, here, east, west):
        at = slice(8 * i, 8 * i + 8)
        north = source[x, 8 * i + 1 : 8 * i + 9]
        south = source[x, 8 * i - 1 : 8 * i + 7]
        return (
            (coef[4, x, at] - around_k(i, k)) * here
            + (coef[0, x, at] + k) * east
            + (coef[1, x, at] + k) * west
            + (coef[2, x, at] + k) * north
            + (coef[3, x, at] + k) * south
        )

    def tiles(step):
        edge = 1 if step == STEPS - 1 else 0
        return range(1 + edge, 1 + tall // 8 - edge)

    for tile in range(STRIPS):
        k = jnp.zeros((1, LANES), F32)
        for s in range(7):
            slice_id = 7 * tile + s
            if slice_id < 2 * levels:
                own = between(iota((1, LANES), 1), 18 * s, 18 * s + 18)
                k = jnp.where(own, spread_ref[slice_id // levels, slice_id % levels], k)
        block = levels + tile // 2
        part = slice((tile % 2) * LANES, (tile % 2 + 1) * LANES)
        for f, dest in enumerate((strip_flow.at[0, 0], strip_flow.at[1, 0], strip_ocean.at[0])):
            dest[before] = rows_low[block, 3 * f : 3 * f + 3, part]
            dest[inner] = fields_ref[f, tile]
            dest[after] = rows_high[block, 3 * f : 3 * f + 3, part]
        close_top(strip_flow.at[1, 0])
        for i in range(1, 1 + tall // 8):
            face = strip_flow[0, 0, 8 * i : 8 * i + 8]
            prepare(0, i, strip_flow, face, pltpu.roll(face, 1, 1))
        here = slice(3 * (tile // 2), 3 * (tile // 2) + 3)
        cells_a[0, 0, before] = below[levels, here, part]
        cells_a[0, 0, inner] = strip_ref[tile]
        cells_a[0, 0, after] = above[levels, here, part]
        source = cells_a.at[0]
        for step in range(STEPS):
            dest = (cells_b, cells_c, None)[step]
            for i in tiles(step):
                at = slice(8 * i, 8 * i + 8)
                value = source[0, at]
                total = update(
                    source, 0, i, k, value, pltpu.roll(value, LANES - 1, 1), pltpu.roll(value, 1, 1)
                )
                if dest is None:
                    patch[tile, 8 * i - 16 : 8 * i - 8] = total
                else:
                    dest[0, 0, at] = total * strip_ocean[0, at]
            source = dest.at[0] if dest is not None else None

    def leave(level):
        return pltpu.make_async_copy(done.at[:, level], out_ref.at[:, level], sems.at[level])

    def one(level, carry):
        flow = flow_all.at[level]
        for group in range(2):

            @pl.when(level == groups[group][0])
            def _():
                for copy in arrivals(group):
                    copy.wait()

        for f in range(2):
            for x in range(2):
                flow[f, x, 0:16] = jnp.zeros((16, LANES), F32)
                flow[f, x, 16 + rows : 32 + rows] = jnp.zeros((16, LANES), F32)
        for x in range(2):
            part = slice(x * LANES, (x + 1) * LANES)
            ocean[x, inner] = ocean_ref[level, x].astype(F32)
            for f, dest in enumerate((flow.at[0, x], flow.at[1, x], ocean.at[x])):
                dest[before] = rows_low[level, 3 * f : 3 * f + 3, part]
                dest[after] = rows_high[level, 3 * f : 3 * f + 3, part]
            close_top(flow.at[1, x])
            for t in range(2):
                cells_a[t, x, before] = below[level, 3 * t : 3 * t + 3, part]
                cells_a[t, x, inner] = state_ref[t * levels + level, x]
                cells_a[t, x, after] = above[level, 3 * t : 3 * t + 3, part]
        for i in range(1, 1 + tall // 8):
            at = slice(8 * i, 8 * i + 8)
            faces = [flow[0, x, at] for x in range(2)]
            turned = [pltpu.roll(v, 1, 1) for v in faces]
            turned[1] = jnp.where(lane == 0, turned[0], turned[1])
            for x in range(2):
                prepare(x, i, flow, faces[x], turned[x])
        ks = [spread_ref[t, level] for t in range(2)]
        spots = [strip_of(t * levels + level) for t in range(2)]
        buffers = (cells_a, cells_b, cells_c)
        for step in range(STEPS):
            for i in tiles(step):
                at = slice(8 * i, 8 * i + 8)
                for t in range(2):
                    source = buffers[step].at[t]
                    here = [source[x, at] for x in range(2)]
                    right = [pltpu.roll(v, LANES - 1, 1) for v in here]
                    left = [pltpu.roll(v, 1, 1) for v in here]
                    east = [jnp.where(lane == LANES - 1, right[1], right[0]), right[1]]
                    west = [left[0], jnp.where(lane == 0, left[0], left[1])]
                    for x in range(2):
                        total = update(source, x, i, ks[t], here[x], east[x], west[x])
                        if step < STEPS - 1:
                            buffers[step + 1][t, x, at] = total * ocean[x, at]
                            continue
                        tile, first = spots[t]
                        shift, keep = (125 - first, lane < 3) if x == 0 else (113 - first, lane >= 125)
                        fixed = turn(patch[tile, 8 * i - 16 : 8 * i - 8], shift)
                        done[t, level, 8 * i - 16 : 8 * i - 8, x * LANES : (x + 1) * LANES] = (
                            jnp.where(keep, fixed, total)
                        )
        leave(level).start()
        return carry

    lax.fori_loop(0, levels, one, 0)
    for level in range(levels):
        leave(level).wait()


def run_steps(where, spread, state, strip, swap_a, swap_b, ef, nf, ocean, fields, low, high):
    levels, rows = ocean.shape[0], ocean.shape[2]
    tall, width = rows + 32, 2 * LANES
    buffer = pltpu.VMEM((2, 2, tall, LANES), F32)
    return pl.pallas_call(
        steps_body,
        name="three_steps",
        out_shape=jax.ShapeDtypeStruct((2, levels, rows, width), F32),
        in_specs=[SMEM, SMEM] + [VMEM] * 4 + [HBM] * 2 + [VMEM] * 4,
        out_specs=HBM,
        scratch_shapes=[
            pltpu.VMEM((levels, 2, 2, tall, LANES), F32),
            pltpu.VMEM((2, tall, LANES), F32),
            pltpu.VMEM((2, 1, tall, LANES), F32),
            pltpu.VMEM((1, tall, LANES), F32),
            pltpu.VMEM((5, 2, tall, LANES), F32),
            buffer,
            buffer,
            buffer,
            pltpu.VMEM((STRIPS, rows, LANES), F32),
            pltpu.VMEM(swap_a.shape, F32),
            pltpu.VMEM(swap_a.shape, F32),
            pltpu.VMEM(low.shape, F32),
            pltpu.VMEM(low.shape, F32),
            pltpu.VMEM((2, levels, rows, width), F32),
            pltpu.SemaphoreType.DMA((levels,)),
            pltpu.SemaphoreType.DMA((4, 2)),
        ],
        compiler_params=pltpu.CompilerParams(vmem_limit_bytes=24 << 20),
    )(where, spread, state, strip, swap_a, swap_b, hbm(ef), hbm(nf), ocean, fields, low, high)


def around(block, axis, distance):
    count = lax.axis_size(axis)
    return lax.ppermute(block, axis, [(i, (i + distance) % count) for i in range(count)])


def swapped(block, axis, start):
    count = lax.axis_size(axis)
    lower = range(start, count - 1, 2)
    return lax.ppermute(block, axis, [(i, i + 1) for i in lower] + [(i + 1, i) for i in lower])


def per_device(
    adjoint_in,
    east_flow,
    north_flow,
    diffusivity,
    land_mask,
    forcing,
    obs_tile,
    obs_block,
    obs_live,
):
    n_lat, n_lon = lax.axis_size("lat"), lax.axis_size("lon")
    lat = lax.axis_index("lat")
    odd = lat % 2
    where = jnp.stack([lat == 0, lat == n_lat - 1, odd == 1]).astype(jnp.int32)
    flat = forcing.transpose(0, 1, 3, 2, 4).reshape(-1, forcing.shape[4])
    packed = pack_records(flat, obs_tile, obs_block, obs_live, n_lat * n_lon, n_lon)
    arrived = lax.all_to_all(packed, ("lat", "lon"), split_axis=0, concat_axis=0, tiled=True)
    columns, ocean = outer_columns(adjoint_in, east_flow, north_flow, land_mask)
    west = around(columns, "lon", 1)
    east = around(columns, "lon", -1)
    own, spread, rest, adj_first, low, high = own_strips(
        east_flow, north_flow, adjoint_in, ocean
    )
    parity = odd.reshape(1).astype(jnp.int32)
    fields, adj_strip, edge_a, edge_b = outer_rows(
        parity, west, east, own, spread, rest, low, high
    )
    edge_a = swapped(edge_a, "lat", 0)
    edge_b = swapped(edge_b, "lat", 1)
    state, strip, swap_a, swap_b = place_records(
        parity, arrived, adj_first, adjoint_in, ocean, adj_strip, fields, spread
    )
    swap_a = swapped(swap_a, "lat", 0)
    swap_b = swapped(swap_b, "lat", 1)
    return run_steps(
        where,
        diffusivity,
        state,
        strip,
        swap_a,
        swap_b,
        east_flow,
        north_flow,
        ocean,
        fields,
        edge_a,
        edge_b,
    )


def solution(mesh):
    in_specs = (
        P(None, None, "lat", "lon"),
        P(None, "lat", "lon"),
        P(None, "lat", "lon"),
        P(),
        P(None, "lat", "lon"),
        P(("lat", "lon"), None, None, None, None),
        P(("lat", "lon"), None),
        P(("lat", "lon"), None),
        P(("lat", "lon")),
    )
    out_specs = P(None, None, "lat", "lon")
    return jax.shard_map(
        per_device, mesh=mesh, in_specs=in_specs, out_specs=out_specs, check_vma=False
    )
```
